512 devices in a mesh: ga: 64 (over z, x), band: 8 (over y, core).
Axes of the slice: x: 4, y: 4, z: 16, core: 2. Of those that a mesh axis runs over, the one named last changes fastest.
Arguments:
- orbitals: bfloat16 [8, 2, 2048, 192], P(None, None, ('ga', 'band')), may hold values from -6 to 6
- projectors: bfloat16 [512, 2, 2048, 192], P(None, None, ('ga', 'band')), may hold values from -0.046875 to 0.046875
- potential: float32 [192, 192, 192], P('ga'), may hold values from -2 to 0.5
- couplings: float32 [512, 512], replicated, may hold values from -3 to 3
- atom_index: int32 [512], replicated, may hold values from 0 to 63
- column_site: int32 [2048], replicated, may hold values from 0 to 36863, as said below
- column_count: int32 [64], replicated, may hold values from 8 to 32, as said below
Outputs:
- applied: float32 [8, 2, 2048, 192], P(None, None, ('ga', 'band'))
The draws below stay inside these ranges and needn't reach their ends.
Inputs may be any that keep to these rules, and one draw needn't show every extreme that they name: `column_site`: distinct positions kx * 192 + ky in the 192 x 192 plane of frequencies. `column_count`: the slot b * 4 + j of band index b in a ga block is used where it lies below that block's count; some ga block has all 32 slots used.
All inputs are finite; a program needn't handle non-finite values.
Results may differ from the reference program's by a relative error of at most 0.0027.
Values may be sent and summed in bfloat16 or wider, within the bound.
A program may use at most 128 MiB of HBM per device.

```python
import jax
import jax.numpy as jnp
from jax import lax

GRID = 192
NPROJ = 512
NATOM = 64
NB = 8
CMAX = 32
NCOLS = 2048
NXY = 36864
N_GA = 64


def draw_column_site(key, part):
    first_key, second_key = jax.random.split(key, 2)
    inner = 1 + jax.random.permutation(first_key, NXY - 2)[:NCOLS - 2]
    ends = jnp.array([0, NXY - 1], dtype=jnp.int32)
    sites = jnp.concatenate([ends, inner.astype(jnp.int32)])
    shuffle = jax.random.permutation(second_key, NCOLS)
    return sites[shuffle].astype(jnp.int32)


def draw_column_count(key, part):
    first_key, second_key = jax.random.split(key, 2)
    lowest = max(1, CMAX // 4)
    counts = jax.random.randint(first_key, (N_GA,), lowest, CMAX + 1)
    shuffle = jax.random.permutation(second_key, N_GA)
    counts = counts.at[shuffle[0]].set(CMAX).at[shuffle[1]].set(lowest)
    return counts.astype(jnp.int32)


def set_ends(values, own_key, smallest, high):
    index_at = [jax.random.randint(jax.random.fold_in(own_key, axis), (), 0, length) for axis, length in enumerate(values.shape)]
    main_axis = values.shape.index(max(values.shape))
    next_to = index_at[:main_axis] + [(index_at[main_axis] + 1) % values.shape[main_axis]] + index_at[main_axis + 1:]
    return values.at[tuple(index_at)].set(smallest).at[tuple(next_to)].set(high)


def steps_of(own_key, shape, pieces, low, largest):
    gain, own = 1.0, jax.random.fold_in(own_key, 6)
    for position, blocks in pieces:
        heights = jnp.exp(jax.random.uniform(jax.random.fold_in(own, position), (blocks,), jnp.float32, low / len(pieces), largest / len(pieces)))
        gain = gain * jnp.repeat(heights, shape[position] // blocks).reshape([-1 if axis == position else 1 for axis in range(len(shape))])
    return gain


def scatter_about(own_key, dims, scale, bound, cuts=(), kind=jnp.bfloat16):
    entries = scale * jax.random.normal(own_key, dims, jnp.float32)
    if cuts:
        entries = entries * steps_of(own_key, dims, cuts, -0.22, 0.18)
    return jnp.clip(entries, -bound, bound).astype(kind)


def setup_inputs(seed: int = 0) -> dict:
    key_of = jax.random.split(jax.random.key(seed), 8)
    orbitals = scatter_about(key_of[0], (NB, 2, NCOLS, GRID), 1.0, 6.0, ((2, 512),))
    projectors = scatter_about(key_of[1], (NPROJ, 2, NCOLS, GRID), ((NCOLS * GRID * NPROJ) ** 0.5) ** -0.5, 0.046875, ((2, 512),))
    potential = jnp.clip(-2.0 + 2.5 * jax.random.uniform(key_of[2], (GRID, GRID, GRID), jnp.float32) ** steps_of(key_of[2], (GRID, GRID, GRID), ((0, 64),), -0.2, 0.2), -2.0, 0.5)
    couplings = scatter_about(key_of[3], (NPROJ, NPROJ), 0.5, 3.0, (), jnp.float32)
    atom_index = set_ends(jax.random.randint(key_of[4], (NPROJ,), 0, NATOM), jax.random.fold_in(key_of[4], 1), 0, NATOM - 1).astype(jnp.int32)
    column_site = draw_column_site(jax.random.fold_in(key_of[7], 71), 0)
    column_count = draw_column_count(jax.random.fold_in(key_of[7], 71), 0)
    return {"orbitals": orbitals, "projectors": projectors, "potential": potential, "couplings": couplings, "atom_index": atom_index, "column_site": column_site, "column_count": column_count}


def reference(orbitals, projectors, potential, couplings, atom_index, column_site, column_count):
    slot_ids = jnp.arange(NCOLS, dtype=jnp.int32)
    active = ((slot_ids % CMAX) < column_count[slot_ids // CMAX]).astype(jnp.float32)
    coefficients = orbitals * active[None, None, :, None].astype(jnp.bfloat16)
    flat_projectors = projectors.reshape(NPROJ * 2, NCOLS * GRID)
    intersections = lax.dot_general(flat_projectors, coefficients.reshape(NB * 2, NCOLS * GRID),
                               (((1,), (1,)), ((), ())), preferred_element_type=jnp.float32)
    intersections = intersections.reshape(NPROJ, 2, NB, 2)
    partial_real = intersections[:, 0, :, 0] + intersections[:, 1, :, 1]
    partial_imag = intersections[:, 0, :, 1] - intersections[:, 1, :, 0]
    summed = jnp.stack([partial_real, partial_imag])
    coupled = jnp.where(atom_index[:, None] == atom_index[None, :], couplings, jnp.zeros_like(couplings))
    weighted = jnp.einsum('pq,cqn->cpn', coupled, summed, precision=lax.Precision.HIGHEST).astype(jnp.bfloat16)
    weight_real = weighted[0].T
    weight_imag = weighted[1].T
    row_real = jnp.stack([weight_real, -weight_imag], axis=-1)
    row_imag = jnp.stack([weight_imag, weight_real], axis=-1)
    mixing = jnp.stack([row_real, row_imag], axis=1).reshape(NB * 2, NPROJ * 2)
    projected = jnp.dot(mixing, flat_projectors, preferred_element_type=jnp.float32).reshape(NB, 2, NCOLS, GRID)
    potential_xyz = jnp.transpose(potential, (1, 2, 0))

    def one_orbital(single):
        values = lax.complex(single[0].astype(jnp.float32), single[1].astype(jnp.float32))
        spectrum = jnp.zeros((GRID * GRID, GRID), values.dtype).at[column_site].set(values)
        spectrum = spectrum.reshape(GRID, GRID, GRID)
        real_field = jnp.fft.ifftn(spectrum) * (GRID ** 3)
        weighted_field = real_field * potential_xyz
        back = jnp.fft.fftn(weighted_field) / (GRID ** 3)
        picked = back.reshape(GRID * GRID, GRID)[column_site]
        return jnp.stack([jnp.real(picked), jnp.imag(picked)])

    local_term = lax.map(one_orbital, coefficients)
    return (local_term + projected) * active[None, None, :, None]
```

```python
import math

import jax
import jax.numpy as jnp
import ml_dtypes
import numpy as np
from jax import lax
from jax.experimental import pallas as pl
from jax.experimental.pallas import tpu as pltpu
from jax.sharding import PartitionSpec as P

MESH = pl.DeviceIdType.MESH
F32 = jnp.float32
BF16 = jnp.bfloat16
GRID = 192
ZN, XN, BN = 16, 4, 8


def split_host(table):
    high = table.astype(ml_dtypes.bfloat16)
    low = (table - high.astype(np.float64)).astype(ml_dtypes.bfloat16)
    return high, low


def make_tables():
    points = np.arange(GRID)
    phases = (points[:, None] * points[None, :] % GRID) * (2.0 * math.pi / GRID)
    order = np.arange(GRID).reshape(2, 4, 3, 8)
    hi, mid, sub, lo = np.meshgrid(np.arange(2), np.arange(4), np.arange(3), np.arange(8), indexing="ij")
    order = (12 * (8 * hi + lo) + 3 * mid + sub).reshape(-1)
    out = []
    for angles in (phases, phases[:, order]):
        cos_h, cos_l = split_host(np.cos(angles))
        sin_h, sin_l = split_host(np.sin(angles))
        out.append(np.concatenate([cos_h, sin_h, cos_l, sin_l], axis=0))
    return out


def dot(left, right):
    return lax.dot_general(left, right, (((1,), (0,)), ((), ())), preferred_element_type=F32)


def dot_nt(left, right):
    return lax.dot_general(left, right, (((1,), (1,)), ((), ())), preferred_element_type=F32)


def split(value):
    high = value.astype(BF16)
    return high, (value - high.astype(F32)).astype(BF16)


def kernel(
    count_ref, site_ref, atom_ref, orb_ref, proj_ref, pot_ref, coup_ref, plane_ref, ztab_ref, out_ref,
    coef, coef_rot, send_b, recv_b, send_pb, recv_pb, turn, send_x, recv_x, send_px, recv_px,
    send_z, recv_z, send_pz, recv_pz, columns, picks_x, picks_y, weights, grid_sum, grid_back,
    coupled_h, coupled_l, back_z, got_z, back_x, got_x, back_px, got_px, back_b, got_b, back_pb, got_pb,
    pairs, wide, sems,
):
    block = lax.axis_index("ga")
    band = lax.axis_index("band")
    zz = block // XN
    xx = block % XN

    def on_band(d):
        return (block, (band + d) % BN), (band + d) % BN

    def on_x(d):
        return (zz * XN + (xx + d) % XN, band), (xx + d) % XN

    def on_z(d):
        return (((zz + d) % ZN) * XN + xx, band), (zz + d) % ZN

    def exchange(first_sem, size, where, source, target):
        def copy(d):
            device, index = where(d)
            return pltpu.make_async_remote_copy(
                src_ref=source(index),
                dst_ref=target,
                send_sem=sems.at[0, first_sem + d],
                recv_sem=sems.at[1, first_sem + d],
                device_id=device,
                device_id_type=MESH,
            )

        def start():
            @pl.loop(1, size)
            def _(d):
                copy(d).start()

        def wait():
            @pl.loop(1, size)
            def _(d):
                copy(d).wait()

        return start, wait

    def rows8(ref, index):
        return ref.at[pl.ds(pl.multiple_of(index * 8, 8), 8)]

    cols_b = exchange(0, BN, on_band, lambda i: send_b.at[i], recv_b.at[band])
    proj_b = exchange(8, BN, on_band, lambda i: rows8(send_pb, i), rows8(recv_pb, band))
    cols_x = exchange(16, XN, on_x, lambda i: send_x.at[i], recv_x.at[xx])
    proj_x = exchange(20, XN, on_x, lambda i: send_px, rows8(recv_px, xx))
    cols_z = exchange(24, ZN, on_z, lambda i: rows8(send_z, i), rows8(recv_z, zz))
    proj_z = exchange(40, ZN, on_z, lambda i: send_pz, rows8(recv_pz, zz))
    sums_x = exchange(56, XN, on_x, lambda i: back_px, rows8(got_px, xx))
    sums_b = exchange(60, BN, on_band, lambda i: back_pb, rows8(got_pb, band))
    home_z = exchange(68, ZN, on_z, lambda i: rows8(back_z, i), rows8(got_z, zz))
    home_x = exchange(84, XN, on_x, lambda i: back_x.at[i], got_x.at[xx])
    home_b = exchange(88, BN, on_band, lambda i: back_b.at[i], got_b.at[band])

    barrier = pltpu.get_barrier_semaphore()
    for size, where in ((ZN, on_z), (XN, on_x), (BN, on_band)):

        @pl.loop(1, size)
        def _(d, where=where):
            pl.semaphore_signal(barrier, inc=1, device_id=where(d)[0], device_id_type=MESH)

    used = count_ref[block]
    row64 = lax.broadcasted_iota(jnp.int32, (64, GRID), 0)
    active = jnp.where(band * 4 + row64 % 4 < used, 1.0, 0.0).astype(F32)
    for n in range(8):
        real = orb_ref[2 * n].astype(F32)
        imag = orb_ref[2 * n + 1].astype(F32)
        coef[8 * n : 8 * n + 4, :] = real
        coef[8 * n + 4 : 8 * n + 8, :] = imag
        coef_rot[8 * n : 8 * n + 4, :] = -imag
        coef_rot[8 * n + 4 : 8 * n + 8, :] = real
    coef[...] = coef[...] * active
    coef_rot[...] = coef_rot[...] * active
    plain = coef[...].astype(BF16)
    rotated = coef_rot[...].astype(BF16)
    along_z = (
        dot(plain, ztab_ref[0:192, :])
        + dot(plain, ztab_ref[384:576, :])
        + dot(rotated, ztab_ref[192:384, :])
        + dot(rotated, ztab_ref[576:768, :])
    )
    send_b[...] = along_z.reshape(8, 8, GRID)

    wide[0, 0:64, :] = coef[:, 0:128]
    wide[1, 0:64, 0:64] = coef[:, 128:192]
    wide[0, 64:128, :] = -coef_rot[:, 0:128]
    wide[1, 64:128, 0:64] = -coef_rot[:, 128:192]

    def slot_rows(start):
        halves = [wide[h, pl.ds(start, 16, stride=4), :] for h in range(2)]
        return jnp.concatenate(halves, axis=1)[:, 0:GRID]

    partial = jnp.zeros((16, 512), F32)
    for slot in range(4):
        left = slot_rows(slot).astype(BF16)
        right = slot_rows(64 + slot).astype(BF16)
        partial += dot(left, proj_ref[slot * 192 : (slot + 1) * 192, :])
        partial += dot(right, proj_ref[(slot + 4) * 192 : (slot + 5) * 192, :])
    for part in range(4):
        send_pb[pl.ds(part, 16, stride=4), :] = partial[:, part * 128 : (part + 1) * 128]

    pl.semaphore_wait(barrier, ZN + XN + BN - 3)
    cols_b[0]()
    proj_b[0]()

    @pl.loop(0, ZN)
    def _(s):
        site = site_ref[pl.ds(s, 1), :]
        kx = (site * 43691) >> 23
        ky = site - kx * 192
        rows = lax.broadcasted_iota(jnp.int32, (GRID, 128), 0)
        lanes = pl.ds(pl.multiple_of(s * 128, 128), 128)
        picks_x[:, lanes] = jnp.where(rows == kx, 1.0, 0.0).astype(BF16)
        picks_y[:, lanes] = jnp.where(rows == ky, 1.0, 0.0).astype(BF16)

    recv_b[pl.ds(band, 1)] = send_b[pl.ds(band, 1)]
    cols_b[1]()
    turn[...] = jnp.zeros_like(turn)
    for b in range(8):
        for c in range(2):
            turn[c * 32 + b * 4 : c * 32 + b * 4 + 4, 0:GRID] = recv_b[b, 4 * c : 4 * c + 4, :]
    turned = turn[...].T
    lane96 = lax.broadcasted_iota(jnp.int32, (96, 128), 1)
    joined = jnp.where(lane96 < 64, turned[0:96], pltpu.roll(turned[96:192], 64, 1))
    send_x[...] = joined.reshape(4, 24, 128)
    cols_x[0]()

    rows8(recv_pb, band)[...] = rows8(send_pb, band)[...]
    proj_b[1]()
    total = recv_pb[0:8, :]
    for b in range(1, 8):
        total += recv_pb[8 * b : 8 * b + 8, :]
    send_px[...] = total
    rows8(recv_px, xx)[...] = total
    proj_x[0]()

    recv_x[pl.ds(xx, 1)] = send_x[pl.ds(xx, 1)]
    cols_x[1]()
    lane24 = lax.broadcasted_iota(jnp.int32, (24, 128), 1)
    for x_lo in range(2):
        low = recv_x[x_lo]
        high = recv_x[x_lo + 2]
        for z_hi in range(2):
            if z_hi == 0:
                pair = jnp.where(lane24 < 64, low, pltpu.roll(high, 64, 1))
            else:
                pair = jnp.where(lane24 < 64, pltpu.roll(low, 64, 1), high)
            for zi in range(3):
                send_z[pl.ds(z_hi * 64 + x_lo * 3 + zi, 8, stride=8), :] = pair[8 * zi : 8 * zi + 8]
                if x_lo == 0 and zi < 2:
                    send_z[pl.ds(z_hi * 64 + 6 + zi, 8, stride=8), :] = jnp.zeros((8, 128), F32)
    cols_z[0]()

    proj_x[1]()
    total = recv_px[0:8, :]
    for x in range(1, 4):
        total += recv_px[8 * x : 8 * x + 8, :]
    grow = lax.broadcasted_iota(jnp.int32, (8, 128), 0)
    mine_r = jnp.sum(jnp.where(grow == xx, total, 0.0), axis=0, keepdims=True)
    mine_i = jnp.sum(jnp.where(grow == xx + 4, total, 0.0), axis=0, keepdims=True)
    mine = jnp.where(grow == 0, mine_r, jnp.where(grow == 1, mine_i, 0.0))
    send_pz[...] = mine
    rows8(recv_pz, zz)[...] = mine
    proj_z[0]()

    atoms = lax.broadcasted_iota(jnp.int32, (64, 128), 0)
    marks = jnp.concatenate(
        [jnp.where(atoms == atom_ref[q : q + 1, :], 1.0, 0.0).astype(F32) for q in range(4)], axis=1
    )
    same = dot(marks.T.astype(BF16), marks.astype(BF16))
    coupled = jnp.where(same > 0.5, coup_ref[...], 0.0)
    part_h, part_l = split(coupled)
    coupled_h[...] = part_h
    coupled_l[...] = part_l

    rows8(recv_z, zz)[...] = rows8(send_z, zz)[...]
    cols_z[1]()
    lane16 = lax.broadcasted_iota(jnp.int32, (16, 128), 1)
    even = (lane16 // 32) % 2 == 0
    for zi in range(3):
        first = recv_z[pl.ds(zi, 16, stride=8), :]
        second = recv_z[pl.ds(zi + 3, 16, stride=8), :]
        columns[zi * 32 : zi * 32 + 16, :] = jnp.where(even, first, pltpu.roll(second, 32, 1))
        columns[zi * 32 + 16 : zi * 32 + 32, :] = jnp.where(even, pltpu.roll(first, 96, 1), second)

    grid_sum[...] = jnp.zeros_like(grid_sum)

    @pl.loop(0, 8)
    def _(t):
        for h in range(2):
            s = 2 * t + h
            spots = picks_x[:, pl.ds(pl.multiple_of(s * 128, 128), 128)]
            for i in range(6):
                value = columns[pl.ds(i * 16 + s, 1), :]
                spread = jnp.broadcast_to(value, (GRID, 128)).astype(BF16)
                weights[i * 192 : (i + 1) * 192, h * 128 : (h + 1) * 128] = spots * spread
        grid_sum[...] += dot_nt(weights[...], picks_y[:, pl.ds(pl.multiple_of(t * 256, 256), 256)])

    proj_z[1]()
    total = recv_pz[0:8, :]
    for z in range(1, 16):
        total += recv_pz[8 * z : 8 * z + 8, :]
    back_px[...] = total
    rows8(got_px, xx)[...] = total
    sums_x[0]()

    table = plane_ref[...]
    cos_h, sin_h, cos_l, sin_l = (table[192 * i : 192 * (i + 1)] for i in range(4))
    scale = 1.0 / float(GRID**3)

    def along_x(value):
        high, low = split(value)
        one = dot(table, high)
        two = dot(table[0:384], low)
        both = one[0:384] + one[384:768] + two
        return both[0:192], both[192:384]

    @pl.loop(0, 3)
    def _(zi):
        rows = pl.ds(pl.multiple_of(zi * 384, 384), 384)
        start = grid_sum[rows, :].astype(BF16)
        by_cos = dot(start, cos_h) + dot(start, cos_l)
        by_sin = dot(start, sin_h) + dot(start, sin_l)
        real_c, real_s = along_x(by_cos[0:192] - by_sin[192:384])
        imag_c, imag_s = along_x(by_sin[0:192] + by_cos[192:384])
        field = pot_ref[zi] * scale
        real_c, real_s, imag_c, imag_s = along_x((real_c - imag_s) * field) + along_x((real_s + imag_c) * field)
        high, low = split(jnp.concatenate([real_c + imag_s, imag_c - real_s], axis=0))
        by_cos = dot(high, cos_h) + dot(high, cos_l) + dot(low, cos_h)
        by_sin = dot(high, sin_h) + dot(high, sin_l) + dot(low, sin_h)
        grid_back[rows, :] = jnp.concatenate(
            [by_cos[0:192] + by_sin[192:384], by_cos[192:384] - by_sin[0:192]], axis=0
        ).astype(BF16)

    sums_x[1]()
    for x in range(4):
        for c in range(2):
            back_pb[c * 4 + x : c * 4 + x + 1, :] = got_px[8 * x + c : 8 * x + c + 1, :]
    rows8(got_pb, band)[...] = back_pb[...]
    sums_b[0]()

    @pl.loop(0, 8)
    def _(t):
        lanes = pl.ds(pl.multiple_of(t * 256, 256), 256)
        picked = dot(grid_back[...], picks_y[:, lanes])
        spots = picks_x[:, lanes].astype(F32)
        for i in range(6):
            value = jnp.sum(picked[i * 192 : (i + 1) * 192] * spots, axis=0, keepdims=True)
            for h in range(2):
                columns[pl.ds(i * 16 + 2 * t + h, 1), :] = value[:, h * 128 : (h + 1) * 128]

    for zi in range(3):
        real = columns[zi * 32 : zi * 32 + 16, :]
        imag = columns[zi * 32 + 16 : zi * 32 + 32, :]
        back_z[pl.ds(zi, 16, stride=8), :] = jnp.where(even, real, pltpu.roll(imag, 32, 1))
        back_z[pl.ds(zi + 3, 16, stride=8), :] = jnp.where(even, pltpu.roll(real, 96, 1), imag)
    for row in (6, 7):
        back_z[pl.ds(row, 16, stride=8), :] = jnp.zeros((16, 128), F32)
    home_z[0]()

    sums_b[1]()
    for part in range(4):
        lanes = slice(part * 128, (part + 1) * 128)
        real = got_pb[pl.ds(part, 8, stride=8), :]
        imag = got_pb[pl.ds(part + 4, 8, stride=8), :]
        pairs[part, pl.ds(0, 8, stride=2), :] = real
        pairs[part, pl.ds(1, 8, stride=2), :] = imag
        pairs[part, pl.ds(16, 8, stride=2), :] = -imag
        pairs[part, pl.ds(17, 8, stride=2), :] = real
    high, low = split(jnp.concatenate([pairs[part] for part in range(4)], axis=1))
    weighted = dot_nt(high, coupled_h[...]) + dot_nt(high, coupled_l[...]) + dot_nt(low, coupled_h[...])
    weighted = weighted.astype(BF16)
    for slot in range(4):
        mixed = dot_nt(weighted[0:16], proj_ref[slot * 192 : (slot + 1) * 192, :]) + dot_nt(
            weighted[16:32], proj_ref[(slot + 4) * 192 : (slot + 5) * 192, :]
        )
        wide[0, pl.ds(slot, 16, stride=4), :] = mixed[:, 0:128]
        wide[1, pl.ds(slot, 16, stride=4), :] = jnp.concatenate([mixed[:, 128:192], jnp.zeros((16, 64), F32)], axis=1)

    rows8(got_z, zz)[...] = rows8(back_z, zz)[...]
    home_z[1]()
    lane8 = lax.broadcasted_iota(jnp.int32, (8, 128), 1)
    for x_lo in range(2):
        for zi in range(3):
            first = got_z[pl.ds(x_lo * 3 + zi, 8, stride=8), :]
            second = got_z[pl.ds(64 + x_lo * 3 + zi, 8, stride=8), :]
            back_x[x_lo, 8 * zi : 8 * zi + 8, :] = jnp.where(lane8 < 64, first, pltpu.roll(second, 64, 1))
            back_x[x_lo + 2, 8 * zi : 8 * zi + 8, :] = jnp.where(lane8 < 64, pltpu.roll(first, 64, 1), second)
    home_x[0]()
    got_x[pl.ds(xx, 1)] = back_x[pl.ds(xx, 1)]
    home_x[1]()
    joined = got_x[...].reshape(96, 128)
    turned = jnp.concatenate([joined, pltpu.roll(joined, 64, 1), jnp.zeros((64, 128), F32)], axis=0).T
    for b in range(8):
        for c in range(2):
            back_b[b, 4 * c : 4 * c + 4, :] = turned[c * 32 + b * 4 : c * 32 + b * 4 + 4, 0:GRID]
    home_b[0]()
    got_b[pl.ds(band, 1)] = back_b[pl.ds(band, 1)]
    home_b[1]()
    for n in range(8):
        coef[8 * n : 8 * n + 4, :] = got_b[n, 0:4, :]
        coef[8 * n + 4 : 8 * n + 8, :] = got_b[n, 4:8, :]
        coef_rot[8 * n : 8 * n + 4, :] = got_b[n, 4:8, :]
        coef_rot[8 * n + 4 : 8 * n + 8, :] = -got_b[n, 0:4, :]
    plain_h, plain_l = split(coef[...])
    rotated_h, rotated_l = split(coef_rot[...])
    local = (
        dot_nt(plain_h, ztab_ref[0:192, :])
        + dot_nt(plain_h, ztab_ref[384:576, :])
        + dot_nt(plain_l, ztab_ref[0:192, :])
        + dot_nt(rotated_h, ztab_ref[192:384, :])
        + dot_nt(rotated_h, ztab_ref[576:768, :])
        + dot_nt(rotated_l, ztab_ref[192:384, :])
    )
    projected = jnp.concatenate([wide[0, 0:64, :], wide[1, 0:64, :]], axis=1)[:, 0:GRID]
    result = (local + projected) * active
    for i in range(16):
        out_ref[i] = result[4 * i : 4 * i + 4, :]


def on_device(orbitals, projectors, potential, couplings, atom_index, column_site, column_count):
    plane, ztab = (jnp.asarray(t) for t in make_tables())
    vmem = pl.BlockSpec(memory_space=pltpu.VMEM)
    smem = pl.BlockSpec(memory_space=pltpu.SMEM)
    flat = projectors.transpose(1, 2, 3, 0).reshape(8 * GRID, 512)
    scratch = lambda *shape: pltpu.VMEM(shape, F32)
    out = pl.pallas_call(
        kernel,
        out_shape=jax.ShapeDtypeStruct((16, 4, GRID), F32),
        in_specs=[smem] + [vmem] * 8,
        out_specs=vmem,
        scratch_shapes=[
            scratch(64, GRID),
            scratch(64, GRID),
            scratch(8, 8, GRID),
            scratch(8, 8, GRID),
            scratch(64, 128),
            scratch(64, 128),
            scratch(128, 256),
            scratch(4, 24, 128),
            scratch(4, 24, 128),
            scratch(8, 128),
            scratch(32, 128),
            scratch(128, 128),
            scratch(128, 128),
            scratch(8, 128),
            scratch(128, 128),
            scratch(96, 128),
            pltpu.VMEM((GRID, 2048), BF16),
            pltpu.VMEM((GRID, 2048), BF16),
            pltpu.VMEM((1152, 256), BF16),
            scratch(1152, GRID),
            pltpu.VMEM((1152, GRID), BF16),
            pltpu.VMEM((512, 512), BF16),
            pltpu.VMEM((512, 512), BF16),
            scratch(128, 128),
            scratch(128, 128),
            scratch(4, 24, 128),
            scratch(4, 24, 128),
            scratch(8, 128),
            scratch(32, 128),
            scratch(8, 8, GRID),
            scratch(8, 8, GRID),
            scratch(8, 128),
            scratch(64, 128),
            scratch(4, 32, 128),
            scratch(2, 128, 128),
            pltpu.SemaphoreType.DMA((2, 96)),
        ],
        compiler_params=pltpu.CompilerParams(
            collective_id=0, has_side_effects=True, vmem_limit_bytes=48 * 1024 * 1024
        ),
    )(
        column_count,
        column_site.reshape(16, 128),
        atom_index.reshape(4, 128),
        orbitals.reshape(16, 4, GRID),
        flat,
        potential,
        couplings,
        plane,
        ztab,
    )
    return out.reshape(8, 2, 4, GRID)


def solution(mesh):
    return jax.shard_map(
        on_device,
        mesh=mesh,
        in_specs=(
            P(None, None, ("ga", "band"), None),
            P(None, None, ("ga", "band"), None),
            P("ga", None, None),
            P(),
            P(),
            P(),
            P(),
        ),
        out_specs=P(None, None, ("ga", "band"), None),
        check_vma=False,
    )
```

```python
import math

import jax
import jax.numpy as jnp
import ml_dtypes
import numpy as np
from jax import lax
from jax.experimental import pallas as pl
from jax.experimental.pallas import tpu as pltpu
from jax.sharding import PartitionSpec as P

MESH = pl.DeviceIdType.MESH
F32 = jnp.float32
BF16 = jnp.bfloat16
GRID = 192
ZN, XN, BN = 16, 4, 8


def split_host(table):
    high = table.astype(ml_dtypes.bfloat16)
    low = (table - high.astype(np.float64)).astype(ml_dtypes.bfloat16)
    return high, low


def make_tables():
    points = np.arange(GRID)
    phases = (points[:, None] * points[None, :] % GRID) * (2.0 * math.pi / GRID)
    lanes = np.full((XN, 128), -1)
    for x in range(XN):
        for sub in range(3):
            lanes[x, 16 * sub : 16 * sub + 16] = 12 * np.arange(ZN) + 3 * x + sub
    lanes = lanes.reshape(-1)
    out = []
    for pick in (points, lanes):
        angles = phases[:, pick]
        cos_h, cos_l = split_host(np.where(pick < 0, 0.0, np.cos(angles)))
        sin_h, sin_l = split_host(np.where(pick < 0, 0.0, np.sin(angles)))
        out.append(np.concatenate([cos_h, sin_h, cos_l, sin_l], axis=0))
    return out


def dot(left, right):
    return lax.dot_general(left, right, (((1,), (0,)), ((), ())), preferred_element_type=F32)


def dot_nt(left, right):
    return lax.dot_general(left, right, (((1,), (1,)), ((), ())), preferred_element_type=F32)


def split(value):
    high = value.astype(BF16)
    return high, (value - high.astype(F32)).astype(BF16)


def kernel(
    count_ref, site_hbm, atom_hbm, orb_hbm, proj_hbm, pot_hbm, coup_hbm, plane_hbm, ztab_hbm, out_ref,
    site_ref, atom_ref, orb_ref, proj_ref, pot_ref, coup_ref, plane_ref, ztab_ref,
    coef, coef_rot, wide, send_b, recv_b, send_pb, recv_pb, turn, stage, send_z, recv_z, send_pz, recv_pz,
    picks_x, picks_y, weights, grid_sum, grid_back, coupled_h, coupled_l, found, back_z, got_z,
    back_b, got_b, back_pb, got_pb, pairs, sems, load_sems,
):
    block = lax.axis_index("ga")
    band = lax.axis_index("band")
    zz = lax.div(block, XN)
    xx = lax.rem(block, XN)
    me = xx * BN + band

    arrays = (
        (orb_hbm, orb_ref), (ztab_hbm, ztab_ref), (proj_hbm, proj_ref), (site_hbm, site_ref),
        (atom_hbm, atom_ref), (coup_hbm, coup_ref), (plane_hbm, plane_ref), (pot_hbm, pot_ref),
    )
    loads = [pltpu.make_async_copy(far, near, load_sems.at[i]) for i, (far, near) in enumerate(arrays)]
    orb_in, ztab_in, proj_in, site_in, atom_in, coup_in, plane_in, pot_in = loads

    def on_plane(d):
        index = lax.rem(me + d, XN * BN)
        return (zz * XN + lax.div(index, BN), lax.rem(index, BN)), index

    def on_z(d):
        index = lax.rem(zz + d, ZN)
        return (index * XN + xx, band), index

    def exchange(first_sem, size, where, source, target):
        def copy(d):
            device, index = where(d)
            return pltpu.make_async_remote_copy(
                src_ref=source(index),
                dst_ref=target,
                send_sem=sems.at[0, first_sem + d],
                recv_sem=sems.at[1, first_sem + d],
                device_id=device,
                device_id_type=MESH,
            )

        def start():
            @pl.loop(1, size)
            def _(d):
                copy(d).start()

        def wait():
            @pl.loop(1, size)
            def _(d):
                copy(d).wait()

        return start, wait, copy

    def rows8(ref, index):
        return ref.at[pl.ds(pl.multiple_of(index * 8, 8), 8)]

    peers = XN * BN
    cols_b = exchange(0, peers, on_plane, lambda i: send_b.at[i], recv_b.at[me])
    proj_b = exchange(32, peers, on_plane, lambda i: rows8(send_pb, i), rows8(recv_pb, me))
    cols_z = exchange(64, ZN, on_z, lambda i: send_z.at[i], recv_z.at[zz])
    proj_z = exchange(80, ZN, on_z, lambda i: send_pz, rows8(recv_pz, zz))
    sums_b = exchange(96, peers, on_plane, lambda i: back_pb, rows8(got_pb, me))
    home_z = exchange(128, ZN, on_z, lambda i: back_z.at[i], got_z.at[zz])
    home_b = exchange(144, peers, on_plane, lambda i: back_b.at[i], got_b.at[me])

    barrier = pltpu.get_barrier_semaphore()
    orb_in.start()
    ztab_in.start()

    @pl.loop(0, ZN - 1)
    def _(i):
        away = lax.rem(i + 8, ZN - 1) + 1
        pl.semaphore_signal(barrier, inc=1, device_id=on_z(away)[0], device_id_type=MESH)

    @pl.loop(1, peers)
    def _(d):
        pl.semaphore_signal(barrier, inc=1, device_id=on_plane(d)[0], device_id_type=MESH)

    for load in loads[2:]:
        load.start()

    used = count_ref[block]
    row64 = lax.broadcasted_iota(jnp.int32, (64, GRID), 0)
    active = jnp.where(band * 4 + row64 % 4 < used, 1.0, 0.0).astype(F32)
    orb_in.wait()
    for n in range(8):
        real = orb_ref[2 * n].astype(F32)
        imag = orb_ref[2 * n + 1].astype(F32)
        coef[8 * n : 8 * n + 4, :] = real
        coef[8 * n + 4 : 8 * n + 8, :] = imag
        coef_rot[8 * n : 8 * n + 4, :] = -imag
        coef_rot[8 * n + 4 : 8 * n + 8, :] = real
    coef[...] = coef[...] * active
    coef_rot[...] = coef_rot[...] * active
    plain = coef[...].astype(BF16)
    rotated = coef_rot[...].astype(BF16)
    ztab_in.wait()
    along_z = (
        dot(plain, ztab_ref[0:192, :])
        + dot(plain, ztab_ref[384:576, :])
        + dot(rotated, ztab_ref[192:384, :])
        + dot(rotated, ztab_ref[576:768, :])
    )
    for x in range(XN):
        send_b[8 * x : 8 * x + 8] = along_z[:, 128 * x : 128 * x + 128].reshape(8, 8, 128).astype(BF16)

    wide[0, 0:64, :] = coef[:, 0:128]
    wide[1, 0:64, 0:64] = coef[:, 128:192]
    wide[0, 64:128, :] = -coef_rot[:, 0:128]
    wide[1, 64:128, 0:64] = -coef_rot[:, 128:192]

    def slot_rows(start):
        parts = [
            jnp.concatenate([wide[h, pl.ds(start + 4 * c, 8, stride=8), :] for h in range(2)], axis=1)
            for c in range(2)
        ]
        return jnp.concatenate(parts, axis=0)[:, 0:GRID].astype(BF16)

    proj_in.wait()
    partial = jnp.zeros((16, 512), F32)
    for slot in range(4):
        partial += dot(slot_rows(slot), proj_ref[slot * 192 : (slot + 1) * 192, :])
        partial += dot(slot_rows(64 + slot), proj_ref[(slot + 4) * 192 : (slot + 5) * 192, :])
    send_pb[...] = jnp.zeros_like(send_pb)
    for x in range(XN):
        for c in range(2):
            send_pb[pl.ds(64 * x + c, 8, stride=8), :] = partial[8 * c : 8 * c + 8, 128 * x : 128 * x + 128]

    pl.semaphore_wait(barrier, ZN + peers - 2)
    cols_b[0]()

    stage[...] = jnp.zeros_like(stage)
    found[...] = jnp.zeros_like(found)
    grid_sum[...] = jnp.zeros_like(grid_sum)
    site_in.wait()

    def sources(t):
        return lax.rem(zz + ZN - t, ZN), lax.rem(zz + t + 1, ZN)

    @pl.loop(0, 8)
    def _(t):
        rows = lax.broadcasted_iota(jnp.int32, (GRID, 128), 0)
        for h, s in enumerate(sources(t)):
            site = site_ref[pl.ds(s, 1), :]
            kx = (site * 43691) >> 23
            ky = site - kx * 192
            lanes = pl.ds(pl.multiple_of(t * 256 + h * 128, 128), 128)
            picks_x[:, lanes] = jnp.where(rows == kx, 1.0, 0.0).astype(BF16)
            picks_y[:, lanes] = jnp.where(rows == ky, 1.0, 0.0).astype(BF16)

    recv_b[pl.ds(me, 1)] = send_b[pl.ds(me, 1)]
    cols_b[1]()
    for x in range(XN):
        for b in range(BN):
            piece = recv_b[8 * x + b].astype(F32)
            row = (x % 2) * 128 + (x // 2) * 64 + b * 4
            turn[row : row + 4, :] = piece[0:4]
            turn[row + 32 : row + 36, :] = piece[4:8]
    for x_lo in range(2):
        turned = turn[128 * x_lo : 128 * x_lo + 128, :].T
        for zi in range(3):
            stage[pl.ds(x_lo * 3 + zi, 16, stride=8), :] = turned[16 * zi : 16 * zi + 16]
    send_z[...] = stage[...].reshape(16, 8, 128).astype(BF16)
    cols_z[0]()
    proj_b[0]()
    recv_z[pl.ds(zz, 1)] = send_z[pl.ds(zz, 1)]

    atom_in.wait()
    coup_in.wait()
    atoms = lax.broadcasted_iota(jnp.int32, (64, 128), 0)
    marks = jnp.concatenate(
        [jnp.where(atoms == atom_ref[q : q + 1, :], 1.0, 0.0).astype(F32) for q in range(4)], axis=1
    )
    same = dot(marks.T.astype(BF16), marks.astype(BF16))
    coupled = jnp.where(same > 0.5, coup_ref[...], 0.0)
    part_h, part_l = split(coupled)
    coupled_h[...] = part_h
    coupled_l[...] = part_l

    lane8 = lax.broadcasted_iota(jnp.int32, (8, 128), 1)
    even = (lane8 // 32) % 2 == 0

    def scatter(t):
        for h, s in enumerate(sources(t)):
            first = recv_z[s].astype(F32)
            second = pltpu.roll(first, 5, 0)
            real = jnp.where(even, first, pltpu.roll(second, 32, 1))
            imag = jnp.where(even, pltpu.roll(first, 96, 1), second)
            spots = picks_x[:, pl.ds(pl.multiple_of(t * 256 + h * 128, 128), 128)]
            for i in range(6):
                value = (real, imag)[i % 2][i // 2 : i // 2 + 1]
                spread = jnp.broadcast_to(value, (GRID, 128)).astype(BF16)
                weights[i * 192 : (i + 1) * 192, h * 128 : (h + 1) * 128] = spots * spread
        grid_sum[...] += dot_nt(weights[...], picks_y[:, pl.ds(pl.multiple_of(t * 256, 256), 256)])

    cols_z[2](15).wait()
    scatter(0)

    rows8(recv_pb, me)[...] = rows8(send_pb, me)[...]
    proj_b[1]()
    total = recv_pb[0:8, :]
    for p in range(1, peers):
        total += recv_pb[8 * p : 8 * p + 8, :]
    send_pz[...] = total
    rows8(recv_pz, zz)[...] = total
    proj_z[0]()

    @pl.loop(1, 8)
    def _(t):
        cols_z[2](t).wait()
        cols_z[2](15 - t).wait()
        scatter(t)

    plane_in.wait()
    pot_in.wait()
    table = plane_ref[...]
    cos_h, sin_h, cos_l, sin_l = (table[192 * i : 192 * (i + 1)] for i in range(4))
    scale = 1.0 / float(GRID**3)

    def along_x(value):
        high, low = split(value)
        one = dot(table, high)
        two = dot(table[0:384], low)
        both = one[0:384] + one[384:768] + two
        return both[0:192], both[192:384]

    def one_plane(zi):
        rows = pl.ds(pl.multiple_of(zi * 384, 384), 384)
        start = grid_sum[rows, :].astype(BF16)
        by_cos = dot(start, cos_h) + dot(start, cos_l)
        by_sin = dot(start, sin_h) + dot(start, sin_l)
        real_c, real_s = along_x(by_cos[0:192] - by_sin[192:384])
        imag_c, imag_s = along_x(by_sin[0:192] + by_cos[192:384])
        field = pot_ref[zi] * scale
        real_c, real_s, imag_c, imag_s = along_x((real_c - imag_s) * field) + along_x((real_s + imag_c) * field)
        high, low = split(jnp.concatenate([real_c + imag_s, imag_c - real_s], axis=0))
        by_cos = dot(high, cos_h) + dot(high, cos_l) + dot(low, cos_h)
        by_sin = dot(high, sin_h) + dot(high, sin_l) + dot(low, sin_h)
        grid_back[rows, :] = jnp.concatenate(
            [by_cos[0:192] + by_sin[192:384], by_cos[192:384] - by_sin[0:192]], axis=0
        ).astype(BF16)

    @pl.loop(0, 2)
    def _(zi):
        one_plane(zi)

    proj_z[1]()
    total = recv_pz[0:8, :]
    for z in range(1, ZN):
        total += recv_pz[8 * z : 8 * z + 8, :]
    back_pb[...] = total
    rows8(got_pb, me)[...] = total
    sums_b[0]()
    one_plane(2)

    row8 = lax.broadcasted_iota(jnp.int32, (8, 128), 0)

    def gather(t):
        lanes = pl.ds(pl.multiple_of(t * 256, 256), 256)
        picked = dot(grid_back[...], picks_y[:, lanes])
        spots = picks_x[:, lanes].astype(F32)
        for i in range(6):
            value = jnp.sum(picked[i * 192 : (i + 1) * 192] * spots, axis=0, keepdims=True)
            for h in range(2):
                found[h * 16 + (i % 2) * 8 + i // 2 : h * 16 + (i % 2) * 8 + i // 2 + 1, :] = value[
                    :, h * 128 : (h + 1) * 128
                ]
        for h, s in enumerate(sources(t)):
            real = found[h * 16 : h * 16 + 8, :]
            imag = found[h * 16 + 8 : h * 16 + 16, :]
            upper = jnp.where(even, real, pltpu.roll(imag, 32, 1))
            lower = jnp.where(even, pltpu.roll(real, 96, 1), imag)
            back_z[s] = jnp.where(row8 < 3, upper, pltpu.roll(lower, 3, 0)).astype(BF16)

    @pl.loop(0, 7)
    def _(i):
        t = 7 - i
        gather(t)
        home_z[2](t + 1).start()
        home_z[2](16 - t).start()

    gather(0)
    home_z[2](1).start()
    got_z[pl.ds(zz, 1)] = back_z[pl.ds(zz, 1)]

    sums_b[1]()
    for part in range(4):
        real = got_pb[pl.ds(64 * part, 8, stride=8), :]
        imag = got_pb[pl.ds(64 * part + 1, 8, stride=8), :]
        pairs[part, pl.ds(0, 8, stride=2), :] = real
        pairs[part, pl.ds(1, 8, stride=2), :] = imag
        pairs[part, pl.ds(16, 8, stride=2), :] = -imag
        pairs[part, pl.ds(17, 8, stride=2), :] = real
    high, low = split(jnp.concatenate([pairs[part] for part in range(4)], axis=1))
    weighted = dot_nt(high, coupled_h[...]) + dot_nt(high, coupled_l[...]) + dot_nt(low, coupled_h[...])
    weighted = weighted.astype(BF16)
    for slot in range(4):
        mixed = dot_nt(weighted[0:16], proj_ref[slot * 192 : (slot + 1) * 192, :]) + dot_nt(
            weighted[16:32], proj_ref[(slot + 4) * 192 : (slot + 5) * 192, :]
        )
        wide[0, pl.ds(slot, 16, stride=4), :] = mixed[:, 0:128]
        wide[1, pl.ds(slot, 16, stride=4), :] = jnp.concatenate([mixed[:, 128:192], jnp.zeros((16, 64), F32)], axis=1)

    home_z[1]()
    stage[...] = got_z[...].astype(F32).reshape(128, 128)
    for x_lo in range(2):
        planes = [stage[pl.ds(x_lo * 3 + zi, 16, stride=8), :] for zi in range(3)]
        turned = jnp.concatenate(planes + [jnp.zeros((80, 128), F32)], axis=0).T
        for x_hi in range(2):
            for b in range(BN):
                row = x_hi * 64 + b * 4
                piece = jnp.concatenate([turned[row : row + 4], turned[row + 32 : row + 36]], axis=0)
                back_b[(x_hi * 2 + x_lo) * 8 + b] = piece.astype(BF16)
    home_b[0]()
    got_b[pl.ds(me, 1)] = back_b[pl.ds(me, 1)]
    home_b[1]()
    wave = jnp.concatenate([got_b[8 * x : 8 * x + 8].astype(F32).reshape(64, 128) for x in range(XN)], axis=1)
    part8 = (lax.broadcasted_iota(jnp.int32, (64, 512), 0) // 4) % 2
    turned = jnp.where(part8 == 0, pltpu.roll(wave, 60, 0), -pltpu.roll(wave, 4, 0)).astype(BF16)
    wave = wave.astype(BF16)
    local = (
        dot_nt(wave, ztab_ref[0:192, :])
        + dot_nt(wave, ztab_ref[384:576, :])
        + dot_nt(turned, ztab_ref[192:384, :])
        + dot_nt(turned, ztab_ref[576:768, :])
    )
    projected = jnp.concatenate([wide[0, 0:64, :], wide[1, 0:64, :]], axis=1)[:, 0:GRID]
    result = (local + projected) * active
    for i in range(16):
        out_ref[i] = result[4 * i : 4 * i + 4, :]


def on_device(orbitals, projectors, potential, couplings, atom_index, column_site, column_count):
    plane, ztab = (jnp.asarray(t) for t in make_tables())
    vmem = pl.BlockSpec(memory_space=pltpu.VMEM)
    hbm = pl.BlockSpec(memory_space=pltpu.HBM)
    smem = pl.BlockSpec(memory_space=pltpu.SMEM)
    flat = projectors.transpose(1, 2, 3, 0).reshape(8 * GRID, 512)
    scratch = lambda *shape: pltpu.VMEM(shape, F32)
    out = pl.pallas_call(
        kernel,
        out_shape=jax.ShapeDtypeStruct((16, 4, GRID), F32),
        in_specs=[smem] + [hbm] * 8,
        out_specs=vmem,
        scratch_shapes=[
            pltpu.VMEM((16, 128), jnp.int32),
            pltpu.VMEM((4, 128), jnp.int32),
            pltpu.VMEM((16, 4, GRID), BF16),
            pltpu.VMEM((8 * GRID, 512), BF16),
            scratch(3, GRID, GRID),
            scratch(512, 512),
            pltpu.VMEM((768, GRID), BF16),
            pltpu.VMEM((768, 512), BF16),
            scratch(64, GRID),
            scratch(64, GRID),
            scratch(2, 128, 128),
            pltpu.VMEM((32, 8, 128), BF16),
            pltpu.VMEM((32, 8, 128), BF16),
            scratch(256, 128),
            scratch(256, 128),
            scratch(256, 128),
            scratch(128, 128),
            pltpu.VMEM((16, 8, 128), BF16),
            pltpu.VMEM((16, 8, 128), BF16),
            scratch(8, 128),
            scratch(128, 128),
            pltpu.VMEM((GRID, 2048), BF16),
            pltpu.VMEM((GRID, 2048), BF16),
            pltpu.VMEM((1152, 256), BF16),
            scratch(1152, GRID),
            pltpu.VMEM((1152, GRID), BF16),
            pltpu.VMEM((512, 512), BF16),
            pltpu.VMEM((512, 512), BF16),
            scratch(32, 128),
            pltpu.VMEM((16, 8, 128), BF16),
            pltpu.VMEM((16, 8, 128), BF16),
            pltpu.VMEM((32, 8, 128), BF16),
            pltpu.VMEM((32, 8, 128), BF16),
            scratch(8, 128),
            scratch(256, 128),
            scratch(4, 32, 128),
            pltpu.SemaphoreType.DMA((2, 176)),
            pltpu.SemaphoreType.DMA((8,)),
        ],
        compiler_params=pltpu.CompilerParams(
            collective_id=0, has_side_effects=True, vmem_limit_bytes=67043328
        ),
    )(
        column_count,
        column_site.reshape(16, 128),
        atom_index.reshape(4, 128),
        orbitals.reshape(16, 4, GRID),
        flat,
        potential,
        couplings,
        plane,
        ztab,
    )
    return out.reshape(8, 2, 4, GRID)


def solution(mesh):
    return jax.shard_map(
        on_device,
        mesh=mesh,
        in_specs=(
            P(None, None, ("ga", "band"), None),
            P(None, None, ("ga", "band"), None),
            P("ga", None, None),
            P(),
            P(),
            P(),
            P(),
        ),
        out_specs=P(None, None, ("ga", "band"), None),
        check_vma=False,
    )
```

```python
import math

import jax
import jax.numpy as jnp
import ml_dtypes
import numpy as np
from jax import lax
from jax.experimental import pallas as pl
from jax.experimental.pallas import tpu as pltpu
from jax.sharding import PartitionSpec as P

MESH = pl.DeviceIdType.MESH
F32 = jnp.float32
BF16 = jnp.bfloat16
GRID = 192
ZN, XN, BN = 16, 4, 8


def split_host(table):
    high = table.astype(ml_dtypes.bfloat16)
    low = (table - high.astype(np.float64)).astype(ml_dtypes.bfloat16)
    return high, low


def make_tables():
    points = np.arange(GRID)
    phases = (points[:, None] * points[None, :] % GRID) * (2.0 * math.pi / GRID)
    lanes = np.full((XN, 128), -1)
    for x in range(XN):
        for sub in range(3):
            lanes[x, 16 * sub : 16 * sub + 16] = 12 * np.arange(ZN) + 3 * x + sub
    lanes = lanes.reshape(-1)
    out = []
    for pick in (points, lanes):
        angles = phases[:, pick]
        cos_h, cos_l = split_host(np.where(pick < 0, 0.0, np.cos(angles)))
        sin_h, sin_l = split_host(np.where(pick < 0, 0.0, np.sin(angles)))
        out.append(np.concatenate([cos_h, sin_h, cos_l, sin_l], axis=0))
    return out


def dot(left, right):
    return lax.dot_general(left, right, (((1,), (0,)), ((), ())), preferred_element_type=F32)


def dot_nt(left, right):
    return lax.dot_general(left, right, (((1,), (1,)), ((), ())), preferred_element_type=F32)


def split(value):
    high = value.astype(BF16)
    return high, (value - high.astype(F32)).astype(BF16)


def kernel(
    count_ref, site_hbm, atom_hbm, orb_hbm, proj_hbm, pot_hbm, coup_hbm, plane_hbm, ztab_hbm, out_ref,
    site_ref, atom_ref, orb_ref, proj_ref, pot_ref, coup_ref, plane_ref, ztab_ref,
    coef, coef_rot, wide, send_b, recv_b, send_pb, recv_pb, turn, stage, send_z, recv_z, send_pz, recv_pz,
    picks_x, picks_y, weights, grid_sum, grid_back, coupled_h, coupled_l, found, back_z, got_z,
    back_b, got_b, back_pb, got_pb, pairs, sems, load_sems,
):
    block = lax.axis_index("ga")
    band = lax.axis_index("band")
    zz = lax.div(block, XN)
    xx = lax.rem(block, XN)
    me = xx * BN + band

    arrays = (
        (orb_hbm, orb_ref), (ztab_hbm, ztab_ref), (proj_hbm, proj_ref), (site_hbm, site_ref),
        (atom_hbm, atom_ref), (coup_hbm, coup_ref), (plane_hbm, plane_ref), (pot_hbm, pot_ref),
    )
    loads = [pltpu.make_async_copy(far, near, load_sems.at[i]) for i, (far, near) in enumerate(arrays)]
    orb_in, ztab_in, proj_in, site_in, atom_in, coup_in, plane_in, pot_in = loads

    def on_plane(d):
        index = lax.rem(me + d, XN * BN)
        return (zz * XN + lax.div(index, BN), lax.rem(index, BN)), index

    def on_z(d):
        index = lax.rem(zz + d, ZN)
        return (index * XN + xx, band), index

    def rows8(ref, index):
        return ref.at[pl.ds(pl.multiple_of(index * 8, 8), 8)]

    peers = XN * BN

    def copy(number, target_of, source, target, arrival=None):
        device, index = target_of
        return pltpu.make_async_remote_copy(
            src_ref=source(index),
            dst_ref=target,
            send_sem=sems.at[2 * number],
            recv_sem=sems.at[2 * number + 1 if arrival is None else arrival],
            device_id=device,
            device_id_type=MESH,
        )

    def exchange(number, size, where, source, target, slots):
        def start_one(d):
            copy(number, where(d), source, target).start()

        def start():
            @pl.loop(0, size)
            def _(i):
                d = lax.rem(i + (20 if size == peers else 8), size)

                @pl.when(d != 0)
                def _():
                    start_one(d)

        def wait():
            every = copy(number, (where(1)[0], 0), lambda i: slots, slots)
            every.wait_send()
            every.wait_recv()

        return start, wait, start_one

    cols_b = exchange(0, peers, on_plane, lambda i: send_b.at[i], recv_b.at[me], recv_b.at[pl.ds(0, peers - 1)])
    proj_b = exchange(
        1, peers, on_plane, lambda i: rows8(send_pb, i), rows8(recv_pb, me), recv_pb.at[pl.ds(0, 8 * peers - 8)]
    )
    proj_z = exchange(2, ZN, on_z, lambda i: send_pz, rows8(recv_pz, zz), recv_pz.at[pl.ds(0, 8 * ZN - 8)])
    sums_b = exchange(3, peers, on_plane, lambda i: back_pb, rows8(got_pb, me), got_pb.at[pl.ds(0, 8 * peers - 8)])
    home_z = exchange(4, ZN, on_z, lambda i: back_z.at[i], got_z.at[zz], got_z.at[pl.ds(0, ZN - 1)])
    home_b = exchange(5, peers, on_plane, lambda i: back_b.at[i], got_b.at[me], got_b.at[pl.ds(0, peers - 1)])

    def cols_z_start():
        def one(d, pair):
            copy(6, on_z(d), lambda i: send_z.at[i], recv_z.at[zz], 14 + pair).start()

        @pl.loop(0, 7)
        def _(i):
            one(8 + i, 7 - i)
            one(7 - i, 7 - i)

        one(15, 0)

    def cols_z_wait(pair, count):
        slots = recv_z.at[pl.ds(0, count)]
        copy(6, (on_z(1)[0], 0), lambda i: slots, slots, 14 + pair).wait_recv()

    def cols_z_sent():
        slots = recv_z.at[pl.ds(0, ZN - 1)]
        copy(6, (on_z(1)[0], 0), lambda i: slots, slots, 14).wait_send()

    barrier = pltpu.get_barrier_semaphore()
    orb_in.start()
    ztab_in.start()

    @pl.loop(0, ZN - 1)
    def _(i):
        away = lax.rem(i + 7, ZN - 1) + 1
        pl.semaphore_signal(barrier, inc=1, device_id=on_z(away)[0], device_id_type=MESH)

    @pl.loop(1, peers)
    def _(d):
        pl.semaphore_signal(barrier, inc=1, device_id=on_plane(d)[0], device_id_type=MESH)

    for load in loads[2:]:
        load.start()

    used = count_ref[block]
    row64 = lax.broadcasted_iota(jnp.int32, (64, GRID), 0)
    active = jnp.where(band * 4 + row64 % 4 < used, 1.0, 0.0).astype(F32)
    orb_in.wait()
    for n in range(8):
        real = orb_ref[2 * n].astype(F32)
        imag = orb_ref[2 * n + 1].astype(F32)
        coef[8 * n : 8 * n + 4, :] = real
        coef[8 * n + 4 : 8 * n + 8, :] = imag
        coef_rot[8 * n : 8 * n + 4, :] = -imag
        coef_rot[8 * n + 4 : 8 * n + 8, :] = real
    coef[...] = coef[...] * active
    coef_rot[...] = coef_rot[...] * active
    plain = coef[...].astype(BF16)
    rotated = coef_rot[...].astype(BF16)
    ztab_in.wait()
    along_z = (
        dot(plain, ztab_ref[0:192, :])
        + dot(plain, ztab_ref[384:576, :])
        + dot(rotated, ztab_ref[192:384, :])
        + dot(rotated, ztab_ref[576:768, :])
    )
    for x in range(XN):
        send_b[8 * x : 8 * x + 8] = along_z[:, 128 * x : 128 * x + 128].reshape(8, 8, 128).astype(BF16)

    wide[0, 0:64, :] = coef[:, 0:128]
    wide[1, 0:64, 0:64] = coef[:, 128:192]
    wide[0, 64:128, :] = -coef_rot[:, 0:128]
    wide[1, 64:128, 0:64] = -coef_rot[:, 128:192]

    def slot_rows(start):
        parts = [
            jnp.concatenate([wide[h, pl.ds(start + 4 * c, 8, stride=8), :] for h in range(2)], axis=1)
            for c in range(2)
        ]
        return jnp.concatenate(parts, axis=0)[:, 0:GRID].astype(BF16)

    proj_in.wait()
    partial = jnp.zeros((16, 512), F32)
    for slot in range(4):
        partial += dot(slot_rows(slot), proj_ref[slot * 192 : (slot + 1) * 192, :])
        partial += dot(slot_rows(64 + slot), proj_ref[(slot + 4) * 192 : (slot + 5) * 192, :])
    send_pb[...] = jnp.zeros_like(send_pb)
    for x in range(XN):
        for c in range(2):
            send_pb[pl.ds(64 * x + c, 8, stride=8), :] = partial[8 * c : 8 * c + 8, 128 * x : 128 * x + 128]

    pl.semaphore_wait(barrier, ZN + peers - 2)
    cols_b[0]()

    stage[...] = jnp.zeros_like(stage)
    found[...] = jnp.zeros_like(found)
    grid_sum[...] = jnp.zeros_like(grid_sum)
    site_in.wait()

    def sources(t):
        return lax.rem(zz + ZN - t, ZN), lax.rem(zz + t + 1, ZN)

    @pl.loop(0, 8)
    def _(t):
        rows = lax.broadcasted_iota(jnp.int32, (GRID, 128), 0)
        for h, s in enumerate(sources(t)):
            site = site_ref[pl.ds(s, 1), :]
            kx = (site * 43691) >> 23
            ky = site - kx * 192
            lanes = pl.ds(pl.multiple_of(t * 256 + h * 128, 128), 128)
            picks_x[:, lanes] = jnp.where(rows == kx, 1.0, 0.0).astype(BF16)
            picks_y[:, lanes] = jnp.where(rows == ky, 1.0, 0.0).astype(BF16)

    recv_b[pl.ds(me, 1)] = send_b[pl.ds(me, 1)]
    cols_b[1]()
    for x in range(XN):
        for b in range(BN):
            piece = recv_b[8 * x + b].astype(F32)
            row = (x % 2) * 128 + (x // 2) * 64 + b * 4
            turn[row : row + 4, :] = piece[0:4]
            turn[row + 32 : row + 36, :] = piece[4:8]
    for x_lo in range(2):
        turned = turn[128 * x_lo : 128 * x_lo + 128, :].T
        for zi in range(3):
            stage[pl.ds(x_lo * 3 + zi, 16, stride=8), :] = turned[16 * zi : 16 * zi + 16]
    send_z[...] = stage[...].reshape(16, 8, 128).astype(BF16)
    cols_z_start()
    proj_b[0]()
    recv_z[pl.ds(zz, 1)] = send_z[pl.ds(zz, 1)]

    atom_in.wait()
    coup_in.wait()
    atoms = lax.broadcasted_iota(jnp.int32, (64, 128), 0)
    marks = jnp.concatenate(
        [jnp.where(atoms == atom_ref[q : q + 1, :], 1.0, 0.0).astype(F32) for q in range(4)], axis=1
    )
    same = dot(marks.T.astype(BF16), marks.astype(BF16))
    coupled = jnp.where(same > 0.5, coup_ref[...], 0.0)
    part_h, part_l = split(coupled)
    coupled_h[...] = part_h
    coupled_l[...] = part_l

    lane8 = lax.broadcasted_iota(jnp.int32, (8, 128), 1)
    even = (lane8 // 32) % 2 == 0

    def scatter(t):
        for h, s in enumerate(sources(t)):
            first = recv_z[s].astype(F32)
            second = pltpu.roll(first, 5, 0)
            real = jnp.where(even, first, pltpu.roll(second, 32, 1))
            imag = jnp.where(even, pltpu.roll(first, 96, 1), second)
            spots = picks_x[:, pl.ds(pl.multiple_of(t * 256 + h * 128, 128), 128)]
            for i in range(6):
                value = (real, imag)[i % 2][i // 2 : i // 2 + 1]
                spread = jnp.broadcast_to(value, (GRID, 128)).astype(BF16)
                weights[i * 192 : (i + 1) * 192, h * 128 : (h + 1) * 128] = spots * spread
        grid_sum[...] += dot_nt(weights[...], picks_y[:, pl.ds(pl.multiple_of(t * 256, 256), 256)])

    cols_z_wait(0, 1)
    scatter(0)

    rows8(recv_pb, me)[...] = rows8(send_pb, me)[...]
    proj_b[1]()
    total = recv_pb[0:8, :]
    for p in range(1, peers):
        total += recv_pb[8 * p : 8 * p + 8, :]
    send_pz[...] = total
    rows8(recv_pz, zz)[...] = total
    proj_z[0]()

    @pl.loop(1, 8)
    def _(t):
        cols_z_wait(t, 2)
        scatter(t)

    cols_z_sent()

    plane_in.wait()
    pot_in.wait()
    table = plane_ref[...]
    cos_h, sin_h, cos_l, sin_l = (table[192 * i : 192 * (i + 1)] for i in range(4))
    scale = 1.0 / float(GRID**3)

    def along_x(value):
        high, low = split(value)
        one = dot(table, high)
        two = dot(table[0:384], low)
        both = one[0:384] + one[384:768] + two
        return both[0:192], both[192:384]

    def one_plane(zi):
        rows = pl.ds(pl.multiple_of(zi * 384, 384), 384)
        start = grid_sum[rows, :].astype(BF16)
        by_cos = dot(start, cos_h) + dot(start, cos_l)
        by_sin = dot(start, sin_h) + dot(start, sin_l)
        real_c, real_s = along_x(by_cos[0:192] - by_sin[192:384])
        imag_c, imag_s = along_x(by_sin[0:192] + by_cos[192:384])
        field = pot_ref[zi] * scale
        real_c, real_s, imag_c, imag_s = along_x((real_c - imag_s) * field) + along_x((real_s + imag_c) * field)
        high, low = split(jnp.concatenate([real_c + imag_s, imag_c - real_s], axis=0))
        by_cos = dot(high, cos_h) + dot(high, cos_l) + dot(low, cos_h)
        by_sin = dot(high, sin_h) + dot(high, sin_l) + dot(low, sin_h)
        grid_back[rows, :] = jnp.concatenate(
            [by_cos[0:192] + by_sin[192:384], by_cos[192:384] - by_sin[0:192]], axis=0
        ).astype(BF16)

    @pl.loop(0, 2)
    def _(zi):
        one_plane(zi)

    proj_z[1]()
    total = recv_pz[0:8, :]
    for z in range(1, ZN):
        total += recv_pz[8 * z : 8 * z + 8, :]
    back_pb[...] = total
    rows8(got_pb, me)[...] = total
    sums_b[0]()
    one_plane(2)

    row8 = lax.broadcasted_iota(jnp.int32, (8, 128), 0)

    def gather(t):
        lanes = pl.ds(pl.multiple_of(t * 256, 256), 256)
        picked = dot(grid_back[...], picks_y[:, lanes])
        spots = picks_x[:, lanes].astype(F32)
        for i in range(6):
            value = jnp.sum(picked[i * 192 : (i + 1) * 192] * spots, axis=0, keepdims=True)
            for h in range(2):
                found[h * 16 + (i % 2) * 8 + i // 2 : h * 16 + (i % 2) * 8 + i // 2 + 1, :] = value[
                    :, h * 128 : (h + 1) * 128
                ]
        for h, s in enumerate(sources(t)):
            real = found[h * 16 : h * 16 + 8, :]
            imag = found[h * 16 + 8 : h * 16 + 16, :]
            upper = jnp.where(even, real, pltpu.roll(imag, 32, 1))
            lower = jnp.where(even, pltpu.roll(real, 96, 1), imag)
            back_z[s] = jnp.where(row8 < 3, upper, pltpu.roll(lower, 3, 0)).astype(BF16)

    @pl.loop(0, 7)
    def _(i):
        t = 7 - i
        gather(t)
        home_z[2](t + 1)
        home_z[2](16 - t)

    gather(0)
    home_z[2](1)
    got_z[pl.ds(zz, 1)] = back_z[pl.ds(zz, 1)]

    sums_b[1]()
    for part in range(4):
        real = got_pb[pl.ds(64 * part, 8, stride=8), :]
        imag = got_pb[pl.ds(64 * part + 1, 8, stride=8), :]
        pairs[part, pl.ds(0, 8, stride=2), :] = real
        pairs[part, pl.ds(1, 8, stride=2), :] = imag
        pairs[part, pl.ds(16, 8, stride=2), :] = -imag
        pairs[part, pl.ds(17, 8, stride=2), :] = real
    high, low = split(jnp.concatenate([pairs[part] for part in range(4)], axis=1))
    weighted = dot_nt(high, coupled_h[...]) + dot_nt(high, coupled_l[...]) + dot_nt(low, coupled_h[...])
    weighted = weighted.astype(BF16)
    for slot in range(4):
        mixed = dot_nt(weighted[0:16], proj_ref[slot * 192 : (slot + 1) * 192, :]) + dot_nt(
            weighted[16:32], proj_ref[(slot + 4) * 192 : (slot + 5) * 192, :]
        )
        wide[0, pl.ds(slot, 16, stride=4), :] = mixed[:, 0:128]
        wide[1, pl.ds(slot, 16, stride=4), :] = jnp.concatenate([mixed[:, 128:192], jnp.zeros((16, 64), F32)], axis=1)

    home_z[1]()
    stage[...] = got_z[...].astype(F32).reshape(128, 128)
    for x_lo in range(2):
        planes = [stage[pl.ds(x_lo * 3 + zi, 16, stride=8), :] for zi in range(3)]
        turned = jnp.concatenate(planes + [jnp.zeros((80, 128), F32)], axis=0).T
        for x_hi in range(2):
            for b in range(BN):
                row = x_hi * 64 + b * 4
                piece = jnp.concatenate([turned[row : row + 4], turned[row + 32 : row + 36]], axis=0)
                back_b[(x_hi * 2 + x_lo) * 8 + b] = piece.astype(BF16)
    home_b[0]()
    got_b[pl.ds(me, 1)] = back_b[pl.ds(me, 1)]
    home_b[1]()
    wave = jnp.concatenate([got_b[8 * x : 8 * x + 8].astype(F32).reshape(64, 128) for x in range(XN)], axis=1)
    part8 = (lax.broadcasted_iota(jnp.int32, (64, 512), 0) // 4) % 2
    turned = jnp.where(part8 == 0, pltpu.roll(wave, 60, 0), -pltpu.roll(wave, 4, 0)).astype(BF16)
    wave = wave.astype(BF16)
    local = (
        dot_nt(wave, ztab_ref[0:192, :])
        + dot_nt(wave, ztab_ref[384:576, :])
        + dot_nt(turned, ztab_ref[192:384, :])
        + dot_nt(turned, ztab_ref[576:768, :])
    )
    projected = jnp.concatenate([wide[0, 0:64, :], wide[1, 0:64, :]], axis=1)[:, 0:GRID]
    result = (local + projected) * active
    for i in range(16):
        out_ref[i] = result[4 * i : 4 * i + 4, :]


def on_device(orbitals, projectors, potential, couplings, atom_index, column_site, column_count):
    plane, ztab = (jnp.asarray(t) for t in make_tables())
    vmem = pl.BlockSpec(memory_space=pltpu.VMEM)
    hbm = pl.BlockSpec(memory_space=pltpu.HBM)
    smem = pl.BlockSpec(memory_space=pltpu.SMEM)
    flat = projectors.transpose(1, 2, 3, 0).reshape(8 * GRID, 512)
    scratch = lambda *shape: pltpu.VMEM(shape, F32)
    out = pl.pallas_call(
        kernel,
        out_shape=jax.ShapeDtypeStruct((16, 4, GRID), F32),
        in_specs=[smem] + [hbm] * 8,
        out_specs=vmem,
        scratch_shapes=[
            pltpu.VMEM((16, 128), jnp.int32),
            pltpu.VMEM((4, 128), jnp.int32),
            pltpu.VMEM((16, 4, GRID), BF16),
            pltpu.VMEM((8 * GRID, 512), BF16),
            scratch(3, GRID, GRID),
            scratch(512, 512),
            pltpu.VMEM((768, GRID), BF16),
            pltpu.VMEM((768, 512), BF16),
            scratch(64, GRID),
            scratch(64, GRID),
            scratch(2, 128, 128),
            pltpu.VMEM((32, 8, 128), BF16),
            pltpu.VMEM((32, 8, 128), BF16),
            scratch(256, 128),
            scratch(256, 128),
            scratch(256, 128),
            scratch(128, 128),
            pltpu.VMEM((16, 8, 128), BF16),
            pltpu.VMEM((16, 8, 128), BF16),
            scratch(8, 128),
            scratch(128, 128),
            pltpu.VMEM((GRID, 2048), BF16),
            pltpu.VMEM((GRID, 2048), BF16),
            pltpu.VMEM((1152, 256), BF16),
            scratch(1152, GRID),
            pltpu.VMEM((1152, GRID), BF16),
            pltpu.VMEM((512, 512), BF16),
            pltpu.VMEM((512, 512), BF16),
            scratch(32, 128),
            pltpu.VMEM((16, 8, 128), BF16),
            pltpu.VMEM((16, 8, 128), BF16),
            pltpu.VMEM((32, 8, 128), BF16),
            pltpu.VMEM((32, 8, 128), BF16),
            scratch(8, 128),
            scratch(256, 128),
            scratch(4, 32, 128),
            pltpu.SemaphoreType.DMA((22,)),
            pltpu.SemaphoreType.DMA((8,)),
        ],
        compiler_params=pltpu.CompilerParams(
            collective_id=0, has_side_effects=True, vmem_limit_bytes=67043328
        ),
    )(
        column_count,
        column_site.reshape(16, 128),
        atom_index.reshape(4, 128),
        orbitals.reshape(16, 4, GRID),
        flat,
        potential,
        couplings,
        plane,
        ztab,
    )
    return out.reshape(8, 2, 4, GRID)


def solution(mesh):
    return jax.shard_map(
        on_device,
        mesh=mesh,
        in_specs=(
            P(None, None, ("ga", "band"), None),
            P(None, None, ("ga", "band"), None),
            P("ga", None, None),
            P(),
            P(),
            P(),
            P(),
        ),
        out_specs=P(None, None, ("ga", "band"), None),
        check_vma=False,
    )
```

```python
import math

import jax
import jax.numpy as jnp
import ml_dtypes
import numpy as np
from jax import lax
from jax.experimental import pallas as pl
from jax.experimental.pallas import tpu as pltpu
from jax.sharding import PartitionSpec as P

MESH = pl.DeviceIdType.MESH
F32 = jnp.float32
BF16 = jnp.bfloat16
GRID = 192
ZN, XN, BN = 16, 4, 8


def split_host(table):
    high = table.astype(ml_dtypes.bfloat16)
    low = (table - high.astype(np.float64)).astype(ml_dtypes.bfloat16)
    return high, low


def make_tables():
    points = np.arange(GRID)
    phases = (points[:, None] * points[None, :] % GRID) * (2.0 * math.pi / GRID)
    down = np.concatenate([np.cos(phases[0:97]), np.sin(phases[1:96])], axis=0)
    plane = np.concatenate(split_host(np.ascontiguousarray(down.T)) + split_host(down), axis=0)
    from_real = np.zeros((GRID, XN, 2, 64))
    from_imag = np.zeros((GRID, XN, 2, 64))
    for x in range(XN):
        for sub in range(3):
            angles = phases[:, 12 * np.arange(ZN) + 3 * x + sub]
            lanes = slice(16 * sub, 16 * sub + 16)
            from_real[:, x, 0, lanes] = np.cos(angles)
            from_real[:, x, 1, lanes] = np.sin(angles)
            from_imag[:, x, 0, lanes] = -np.sin(angles)
            from_imag[:, x, 1, lanes] = np.cos(angles)
    real_h, real_l = split_host(from_real.reshape(GRID, 512))
    imag_h, imag_l = split_host(from_imag.reshape(GRID, 512))
    return plane, np.concatenate([real_h, imag_h, real_l, imag_l], axis=0)


def dot(left, right):
    return lax.dot_general(left, right, (((1,), (0,)), ((), ())), preferred_element_type=F32)


def dot_nt(left, right):
    return lax.dot_general(left, right, (((1,), (1,)), ((), ())), preferred_element_type=F32)


def split(value):
    high = value.astype(BF16)
    return high, (value - high.astype(F32)).astype(BF16)


def kernel(
    count_ref, site_hbm, atom_hbm, orb_hbm, proj_hbm, pot_hbm, coup_hbm, plane_hbm, ztab_hbm, out_ref,
    site_ref, atom_ref, orb_ref, proj_ref, pot_ref, coup_ref, plane_ref, ztab_ref,
    wide, send_b, recv_b, send_pb, recv_pb, turn, stage, send_z, recv_z, send_pz, recv_pz,
    picks_x, picks_y, weights, grid_sum, grid_back, coupled_h, coupled_l, found, back_z, got_z,
    back_b, got_b, back_pb, got_pb, sems, load_sems,
):
    block = lax.axis_index("ga")
    band = lax.axis_index("band")
    zz = lax.div(block, XN)
    xx = lax.rem(block, XN)
    me = xx * BN + band

    arrays = (
        (orb_hbm, orb_ref), (ztab_hbm, ztab_ref), (proj_hbm, proj_ref), (site_hbm, site_ref),
        (atom_hbm, atom_ref), (coup_hbm, coup_ref), (plane_hbm, plane_ref), (pot_hbm, pot_ref),
    )
    loads = [pltpu.make_async_copy(far, near, load_sems.at[i]) for i, (far, near) in enumerate(arrays)]
    orb_in, ztab_in, proj_in, site_in, atom_in, coup_in, plane_in, pot_in = loads

    def on_plane(d):
        index = lax.rem(me + d, XN * BN)
        return (zz * XN + lax.div(index, BN), lax.rem(index, BN)), index

    def on_z(d):
        index = lax.rem(zz + d, ZN)
        return (index * XN + xx, band), index

    def rows8(ref, index):
        return ref.at[pl.ds(pl.multiple_of(index * 8, 8), 8)]

    peers = XN * BN

    def copy(number, target_of, source, target, arrival=None):
        device, index = target_of
        return pltpu.make_async_remote_copy(
            src_ref=source(index),
            dst_ref=target,
            send_sem=sems.at[2 * number],
            recv_sem=sems.at[2 * number + 1 if arrival is None else arrival],
            device_id=device,
            device_id_type=MESH,
        )

    def exchange(number, size, where, source, target, slots):
        def start_one(d):
            copy(number, where(d), source, target).start()

        def start():
            @pl.loop(0, size)
            def _(i):
                d = lax.rem(i + (20 if size == peers else 8), size)

                @pl.when(d != 0)
                def _():
                    start_one(d)

        def wait():
            every = copy(number, (where(1)[0], 0), lambda i: slots, slots)
            every.wait_send()
            every.wait_recv()

        return start, wait, start_one

    cols_b = exchange(0, peers, on_plane, lambda i: send_b.at[i], recv_b.at[me], recv_b.at[pl.ds(0, peers - 1)])
    proj_b = exchange(
        1, peers, on_plane, lambda i: rows8(send_pb, i), rows8(recv_pb, me), recv_pb.at[pl.ds(0, 8 * peers - 8)]
    )
    proj_z = exchange(2, ZN, on_z, lambda i: send_pz, rows8(recv_pz, zz), recv_pz.at[pl.ds(0, 8 * ZN - 8)])
    sums_b = exchange(3, peers, on_plane, lambda i: back_pb, rows8(got_pb, me), got_pb.at[pl.ds(0, 8 * peers - 8)])
    home_z = exchange(4, ZN, on_z, lambda i: back_z.at[i], got_z.at[zz], got_z.at[pl.ds(0, ZN - 1)])
    home_b = exchange(5, peers, on_plane, lambda i: back_b.at[i], got_b.at[me], got_b.at[pl.ds(0, peers - 1)])

    def cols_z_start():
        def one(d, pair):
            copy(6, on_z(d), lambda i: send_z.at[i], recv_z.at[zz], 14 + pair).start()

        @pl.loop(0, 7)
        def _(i):
            one(8 + i, 7 - i)
            one(7 - i, 7 - i)

        one(15, 0)

    def cols_z_wait(pair, count):
        slots = recv_z.at[pl.ds(0, count)]
        copy(6, (on_z(1)[0], 0), lambda i: slots, slots, 14 + pair).wait_recv()

    def cols_z_sent():
        slots = recv_z.at[pl.ds(0, ZN - 1)]
        copy(6, (on_z(1)[0], 0), lambda i: slots, slots, 14).wait_send()

    barrier = pltpu.get_barrier_semaphore()
    orb_in.start()
    ztab_in.start()

    @pl.loop(0, ZN - 1)
    def _(i):
        away = lax.rem(i + 7, ZN - 1) + 1
        pl.semaphore_signal(barrier, inc=1, device_id=on_z(away)[0], device_id_type=MESH)

    @pl.loop(1, peers)
    def _(d):
        pl.semaphore_signal(barrier, inc=1, device_id=on_plane(d)[0], device_id_type=MESH)

    for load in loads[2:]:
        load.start()

    used = count_ref[block]
    row32 = lax.broadcasted_iota(jnp.int32, (32, GRID), 0)
    active = jnp.where(band * 4 + row32 % 4 < used, 1.0, 0.0).astype(F32)
    orb_in.wait()
    for n in range(8):
        for c in range(2):
            piece = orb_ref[2 * n + c].astype(F32)
            wide[0, 32 * c + 4 * n : 32 * c + 4 * n + 4, :] = piece[:, 0:128]
            wide[1, 32 * c + 4 * n : 32 * c + 4 * n + 4, 0:64] = piece[:, 128:192]

    def wide_rows(rows):
        return jnp.concatenate([wide[h, rows, :] for h in range(2)], axis=1)[:, 0:GRID]

    real = wide_rows(slice(0, 32)) * active
    imag = wide_rows(slice(32, 64)) * active
    for start, part in ((0, real), (32, imag), (64, -real)):
        wide[0, start : start + 32, :] = part[:, 0:128]
        wide[1, start : start + 32, 0:64] = part[:, 128:192]
    real = real.astype(BF16)
    imag = imag.astype(BF16)
    ztab_in.wait()
    along_z = (
        dot(real, ztab_ref[0:192, :])
        + dot(real, ztab_ref[384:576, :])
        + dot(imag, ztab_ref[192:384, :])
        + dot(imag, ztab_ref[576:768, :])
    )
    for x in range(XN):
        for n in range(8):
            send_b[8 * x + n] = along_z[4 * n : 4 * n + 4, 128 * x : 128 * x + 128].astype(BF16)

    def slot_rows(slot, starts):
        parts = [wide_rows(pl.ds(start + slot, 8, stride=4)) for start in starts]
        return jnp.concatenate(parts, axis=0).astype(BF16)

    proj_in.wait()
    partial = jnp.zeros((16, 512), F32)
    for slot in range(4):
        partial += dot(slot_rows(slot, (0, 32)), proj_ref[slot * 192 : (slot + 1) * 192, :])
        partial += dot(slot_rows(slot, (32, 64)), proj_ref[(slot + 4) * 192 : (slot + 5) * 192, :])
    send_pb[...] = jnp.zeros_like(send_pb)
    for x in range(XN):
        for c in range(2):
            send_pb[pl.ds(64 * x + c, 8, stride=8), :] = partial[8 * c : 8 * c + 8, 128 * x : 128 * x + 128]

    pl.semaphore_wait(barrier, ZN + peers - 2)
    cols_b[0]()

    stage[...] = jnp.zeros_like(stage)
    found[...] = jnp.zeros_like(found)
    grid_sum[...] = jnp.zeros_like(grid_sum)
    site_in.wait()

    def sources(t):
        return lax.rem(zz + ZN - t, ZN), lax.rem(zz + t + 1, ZN)

    rows = lax.broadcasted_iota(jnp.int32, (GRID, 128), 0)
    is_even = rows < 97
    frequency = jnp.where(is_even, rows, rows - 96)

    def folded(position):
        distance = jnp.minimum(position, GRID - position)
        sign = jnp.where(position < 96, 1.0, -1.0).astype(F32)
        return jnp.where(frequency == distance, jnp.where(is_even, 1.0, sign), 0.0).astype(BF16)

    @pl.loop(0, 8)
    def _(t):
        for h, s in enumerate(sources(t)):
            site = site_ref[pl.ds(s, 1), :]
            kx = (site * 43691) >> 23
            lanes = pl.ds(pl.multiple_of(t * 256 + h * 128, 128), 128)
            picks_x[:, lanes] = folded(kx)
            picks_y[:, lanes] = folded(site - kx * 192)

    recv_b[pl.ds(me, 1)] = send_b[pl.ds(me, 1)]
    cols_b[1]()
    for p in range(peers):
        turn[4 * p : 4 * p + 4, :] = recv_b[p].astype(F32)
    turned = turn[...].T
    for c in range(2):
        for zi in range(3):
            stage[pl.ds(c * 3 + zi, 16, stride=8), :] = turned[64 * c + 16 * zi : 64 * c + 16 * zi + 16]
    send_z[...] = stage[...].reshape(16, 8, 128).astype(BF16)
    cols_z_start()
    proj_b[0]()
    recv_z[pl.ds(zz, 1)] = send_z[pl.ds(zz, 1)]

    atom_in.wait()
    coup_in.wait()
    atoms = lax.broadcasted_iota(jnp.int32, (64, 128), 0)
    marks = jnp.concatenate(
        [jnp.where(atoms == atom_ref[q : q + 1, :], 1.0, 0.0).astype(F32) for q in range(4)], axis=1
    )
    same = dot(marks.T.astype(BF16), marks.astype(BF16))
    coupled = jnp.where(same > 0.5, coup_ref[...], 0.0)
    part_h, part_l = split(coupled)
    coupled_h[...] = part_h
    coupled_l[...] = part_l

    def scatter(t):
        for h, s in enumerate(sources(t)):
            arrived = recv_z[s].astype(F32)
            spots = picks_x[:, pl.ds(pl.multiple_of(t * 256 + h * 128, 128), 128)]
            for i in range(6):
                row = (i % 2) * 3 + i // 2
                value = arrived[row : row + 1]
                spread = jnp.broadcast_to(value, (GRID, 128)).astype(BF16)
                weights[i * 192 : (i + 1) * 192, h * 128 : (h + 1) * 128] = spots * spread
        grid_sum[...] += dot_nt(weights[...], picks_y[:, pl.ds(pl.multiple_of(t * 256, 256), 256)])

    cols_z_wait(0, 1)
    scatter(0)

    rows8(recv_pb, me)[...] = rows8(send_pb, me)[...]
    proj_b[1]()
    total = recv_pb[0:8, :]
    for p in range(1, peers):
        total += recv_pb[8 * p : 8 * p + 8, :]
    send_pz[...] = total
    rows8(recv_pz, zz)[...] = total
    proj_z[0]()

    @pl.loop(1, 8)
    def _(t):
        cols_z_wait(t, 2)
        scatter(t)

    cols_z_sent()

    plane_in.wait()
    pot_in.wait()
    across_h = plane_ref[0:192, :]
    across_l = plane_ref[192:384, :]
    down_h = plane_ref[384:576, :]
    down_l = plane_ref[576:768, :]
    scale = 1.0 / float(GRID**3)
    even_row = lax.broadcasted_iota(jnp.int32, (GRID, GRID), 0) < 97
    even_lane = lax.broadcasted_iota(jnp.int32, (GRID, GRID), 1) < 97

    def times_i(even, real, imag):
        return jnp.where(even, real, -imag), jnp.where(even, imag, real)

    def times_minus_i(even, real, imag):
        return jnp.where(even, real, imag), jnp.where(even, imag, -real)

    def from_left(first, value):
        high, low = split(value)
        both = dot(plane_ref[first : first + 384, :], high)
        return both[0:192] + both[192:384] + dot(plane_ref[first : first + 192, :], low)

    def from_right(real, imag, table_h, table_l):
        high, low = split(jnp.concatenate([real, imag], axis=0))
        both = dot(high, table_h) + dot(high, table_l) + dot(low, table_h)
        return both[0:192], both[192:384]

    def one_plane(zi):
        rows = pl.ds(pl.multiple_of(zi * 384, 384), 384)
        start = grid_sum[rows, :]
        real, imag = times_i(even_lane, start[0:192], start[192:384])
        real, imag = from_right(real, imag, down_h, down_l)
        real, imag = times_i(even_row, real, imag)
        field = pot_ref[zi] * scale
        real = from_left(0, real) * field
        imag = from_left(0, imag) * field
        real = from_left(384, real)
        imag = from_left(384, imag)
        real, imag = times_minus_i(even_row, real, imag)
        real, imag = from_right(real, imag, across_h, across_l)
        real, imag = times_minus_i(even_lane, real, imag)
        grid_back[rows, :] = jnp.concatenate([real, imag], axis=0).astype(BF16)

    @pl.loop(0, 2)
    def _(zi):
        one_plane(zi)

    proj_z[1]()
    total = recv_pz[0:8, :]
    for z in range(1, ZN):
        total += recv_pz[8 * z : 8 * z + 8, :]
    back_pb[...] = total
    rows8(got_pb, me)[...] = total
    sums_b[0]()
    one_plane(2)

    def gather(t):
        lanes = pl.ds(pl.multiple_of(t * 256, 256), 256)
        picked = dot(grid_back[...], picks_y[:, lanes])
        spots = picks_x[:, lanes].astype(F32)
        for i in range(6):
            value = jnp.sum(picked[i * 192 : (i + 1) * 192] * spots, axis=0, keepdims=True)
            for h in range(2):
                row = h * 8 + (i % 2) * 3 + i // 2
                found[row : row + 1, :] = value[:, h * 128 : (h + 1) * 128]
        for h, s in enumerate(sources(t)):
            back_z[s] = found[8 * h : 8 * h + 8, :]

    @pl.loop(0, 7)
    def _(i):
        t = 7 - i
        gather(t)
        home_z[2](t + 1)
        home_z[2](16 - t)

    gather(0)
    home_z[2](1)
    got_z[pl.ds(zz, 1)] = back_z[pl.ds(zz, 1)]

    sums_b[1]()
    pairs = []
    for part in range(4):
        real = got_pb[pl.ds(64 * part, 8, stride=8), :]
        imag = got_pb[pl.ds(64 * part + 1, 8, stride=8), :]
        pairs.append(jnp.concatenate([real, imag, -imag, real], axis=0))
    high, low = split(jnp.concatenate(pairs, axis=1))
    weighted = dot_nt(high, coupled_h[...]) + dot_nt(high, coupled_l[...]) + dot_nt(low, coupled_h[...])
    weighted = weighted.astype(BF16)
    for slot in range(4):
        mixed = dot_nt(weighted[0:16], proj_ref[slot * 192 : (slot + 1) * 192, :]) + dot_nt(
            weighted[16:32], proj_ref[(slot + 4) * 192 : (slot + 5) * 192, :]
        )
        mixed = jnp.concatenate([mixed, jnp.zeros((16, 64), F32)], axis=1)
        for c in range(2):
            for h in range(2):
                wide[h, pl.ds(32 * c + slot, 8, stride=4), :] = mixed[8 * c : 8 * c + 8, 128 * h : 128 * h + 128]

    home_z[1]()
    stage[...] = got_z[...].reshape(128, 128)
    rows = []
    for c in range(2):
        rows += [stage[pl.ds(c * 3 + zi, 16, stride=8), :] for zi in range(3)]
        rows.append(jnp.zeros((16, 128), F32))
    turned = jnp.concatenate(rows, axis=0).T
    for p in range(peers):
        back_b[p] = turned[4 * p : 4 * p + 4]
    home_b[0]()
    got_b[pl.ds(me, 1)] = back_b[pl.ds(me, 1)]
    home_b[1]()
    for x in range(XN):
        for n in range(8):
            turn[32 * x + 4 * n : 32 * x + 4 * n + 4, :] = got_b[8 * x + n]
    wave = jnp.concatenate([turn[32 * x : 32 * x + 32, :] for x in range(XN)], axis=1)
    high, low = split(wave)
    for c in range(2):
        table_h = ztab_ref[192 * c : 192 * c + 192, :]
        local = dot_nt(high, table_h) + dot_nt(high, ztab_ref[192 * c + 384 : 192 * c + 576, :]) + dot_nt(low, table_h)
        result = (local + wide_rows(slice(32 * c, 32 * c + 32))) * active
        for n in range(8):
            out_ref[2 * n + c] = result[4 * n : 4 * n + 4, :]


def on_device(orbitals, projectors, potential, couplings, atom_index, column_site, column_count):
    plane, ztab = (jnp.asarray(t) for t in make_tables())
    vmem = pl.BlockSpec(memory_space=pltpu.VMEM)
    hbm = pl.BlockSpec(memory_space=pltpu.HBM)
    smem = pl.BlockSpec(memory_space=pltpu.SMEM)
    flat = projectors.transpose(1, 2, 3, 0).reshape(8 * GRID, 512)
    scratch = lambda *shape: pltpu.VMEM(shape, F32)
    out = pl.pallas_call(
        kernel,
        out_shape=jax.ShapeDtypeStruct((16, 4, GRID), F32),
        in_specs=[smem] + [hbm] * 8,
        out_specs=vmem,
        scratch_shapes=[
            pltpu.VMEM((16, 128), jnp.int32),
            pltpu.VMEM((4, 128), jnp.int32),
            pltpu.VMEM((16, 4, GRID), BF16),
            pltpu.VMEM((8 * GRID, 512), BF16),
            scratch(3, GRID, GRID),
            scratch(512, 512),
            pltpu.VMEM((768, GRID), BF16),
            pltpu.VMEM((768, 512), BF16),
            scratch(2, 128, 128),
            pltpu.VMEM((32, 4, 128), BF16),
            pltpu.VMEM((32, 4, 128), BF16),
            scratch(256, 128),
            scratch(256, 128),
            scratch(128, 128),
            scratch(128, 128),
            pltpu.VMEM((16, 8, 128), BF16),
            pltpu.VMEM((16, 8, 128), BF16),
            scratch(8, 128),
            scratch(128, 128),
            pltpu.VMEM((GRID, 2048), BF16),
            pltpu.VMEM((GRID, 2048), BF16),
            pltpu.VMEM((1152, 256), BF16),
            scratch(1152, GRID),
            pltpu.VMEM((1152, GRID), BF16),
            pltpu.VMEM((512, 512), BF16),
            pltpu.VMEM((512, 512), BF16),
            scratch(16, 128),
            scratch(16, 8, 128),
            scratch(16, 8, 128),
            scratch(32, 4, 128),
            scratch(32, 4, 128),
            scratch(8, 128),
            scratch(256, 128),
            pltpu.SemaphoreType.DMA((22,)),
            pltpu.SemaphoreType.DMA((8,)),
        ],
        compiler_params=pltpu.CompilerParams(
            collective_id=0, has_side_effects=True, vmem_limit_bytes=67043328
        ),
    )(
        column_count,
        column_site.reshape(16, 128),
        atom_index.reshape(4, 128),
        orbitals.reshape(16, 4, GRID),
        flat,
        potential,
        couplings,
        plane,
        ztab,
    )
    return out.reshape(8, 2, 4, GRID)


def solution(mesh):
    return jax.shard_map(
        on_device,
        mesh=mesh,
        in_specs=(
            P(None, None, ("ga", "band"), None),
            P(None, None, ("ga", "band"), None),
            P("ga", None, None),
            P(),
            P(),
            P(),
            P(),
        ),
        out_specs=P(None, None, ("ga", "band"), None),
        check_vma=False,
    )
```

```python
import math

import jax
import jax.numpy as jnp
import ml_dtypes
import numpy as np
from jax import lax
from jax.experimental import pallas as pl
from jax.experimental.pallas import tpu as pltpu
from jax.sharding import PartitionSpec as P

MESH = pl.DeviceIdType.MESH
F32 = jnp.float32
BF16 = jnp.bfloat16
GRID = 192
ZN, XN, BN = 16, 4, 8
FAR_FIRST = {
    ZN: [8, 9, 7, 10, 6, 11, 5, 12, 4, 13, 3, 14, 2, 15, 1],
    XN * BN: [d % 32 for d in range(20, 52) if d != 32],
}


def split_host(table):
    high = table.astype(ml_dtypes.bfloat16)
    low = (table - high.astype(np.float64)).astype(ml_dtypes.bfloat16)
    return high, low


def make_tables():
    points = np.arange(GRID)
    phases = (points[:, None] * points[None, :] % GRID) * (2.0 * math.pi / GRID)
    down = np.concatenate([np.cos(phases[0:97]), np.sin(phases[1:96])], axis=0)
    plane = np.concatenate(split_host(np.ascontiguousarray(down.T)) + split_host(down), axis=0)
    from_real = np.zeros((GRID, XN, 2, 64))
    from_imag = np.zeros((GRID, XN, 2, 64))
    for x in range(XN):
        for sub in range(3):
            angles = phases[:, 12 * np.arange(ZN) + 3 * x + sub]
            lanes = slice(16 * sub, 16 * sub + 16)
            from_real[:, x, 0, lanes] = np.cos(angles)
            from_real[:, x, 1, lanes] = np.sin(angles)
            from_imag[:, x, 0, lanes] = -np.sin(angles)
            from_imag[:, x, 1, lanes] = np.cos(angles)
    real_h, real_l = split_host(from_real.reshape(GRID, 512))
    imag_h, imag_l = split_host(from_imag.reshape(GRID, 512))
    return plane, np.concatenate([real_h, imag_h, real_l, imag_l], axis=0)


def dot(left, right):
    return lax.dot_general(left, right, (((1,), (0,)), ((), ())), preferred_element_type=F32)


def dot_nt(left, right):
    return lax.dot_general(left, right, (((1,), (1,)), ((), ())), preferred_element_type=F32)


def split(value):
    high = value.astype(BF16)
    return high, (value - high.astype(F32)).astype(BF16)


def kernel(
    count_ref, site_hbm, atom_hbm, orb_hbm, proj_hbm, pot_hbm, coup_hbm, plane_hbm, ztab_hbm, out_ref,
    site_ref, atom_ref, orb_ref, proj_ref, pot_ref, coup_ref, plane_ref, ztab_ref,
    wide, send_b, recv_b, send_pb, recv_pb, turn, stage, send_z, recv_z, send_pz, recv_pz,
    picks_x, picks_y, weights, grid_sum, grid_back, coupled_h, coupled_l, found, back_z, got_z,
    back_b, got_b, back_pb, got_pb, sems, load_sems,
):
    block = lax.axis_index("ga")
    band = lax.axis_index("band")
    zz = lax.div(block, XN)
    xx = lax.rem(block, XN)
    me = xx * BN + band

    arrays = (
        (orb_hbm, orb_ref), (ztab_hbm, ztab_ref), (proj_hbm, proj_ref), (site_hbm, site_ref),
        (atom_hbm, atom_ref), (coup_hbm, coup_ref), (plane_hbm, plane_ref), (pot_hbm, pot_ref),
    )
    loads = [pltpu.make_async_copy(far, near, load_sems.at[i]) for i, (far, near) in enumerate(arrays)]
    orb_in, ztab_in, proj_in, site_in, atom_in, coup_in, plane_in, pot_in = loads

    def on_plane(d):
        index = lax.rem(me + d, XN * BN)
        return (zz * XN + lax.div(index, BN), lax.rem(index, BN)), index

    def on_z(d):
        index = lax.rem(zz + d, ZN)
        return (index * XN + xx, band), index

    peers = XN * BN

    def copy(number, target_of, source, target, arrival=None):
        device, index = target_of
        return pltpu.make_async_remote_copy(
            src_ref=source(index),
            dst_ref=target,
            send_sem=sems.at[2 * number],
            recv_sem=sems.at[2 * number + 1 if arrival is None else arrival],
            device_id=device,
            device_id_type=MESH,
        )

    def exchange(number, size, where, source, target, slots):
        def start_one(d):
            copy(number, where(d), source, target).start()

        def start():
            for d in FAR_FIRST[size]:
                start_one(d)

        def wait():
            every = copy(number, (where(1)[0], 0), lambda i: slots, slots)
            every.wait_send()
            every.wait_recv()

        return start, wait, start_one

    cols_b = exchange(0, peers, on_plane, lambda i: send_b.at[i], recv_b.at[me], recv_b.at[pl.ds(0, peers - 1)])
    proj_b = exchange(1, peers, on_plane, lambda i: send_pb.at[i], recv_pb.at[me], recv_pb.at[pl.ds(0, peers - 1)])
    proj_z = exchange(2, ZN, on_z, lambda i: send_pz, recv_pz.at[zz], recv_pz.at[pl.ds(0, ZN - 1)])
    sums_b = exchange(3, peers, on_plane, lambda i: back_pb, got_pb.at[me], got_pb.at[pl.ds(0, peers - 1)])
    home_z = exchange(4, ZN, on_z, lambda i: back_z.at[i], got_z.at[zz], got_z.at[pl.ds(0, ZN - 1)])
    home_b = exchange(5, peers, on_plane, lambda i: back_b.at[i], got_b.at[me], got_b.at[pl.ds(0, peers - 1)])

    def cols_z_start():
        def one(d, pair):
            copy(6, on_z(d), lambda i: send_z.at[i], recv_z.at[zz], 14 + pair).start()

        for pair in range(7, 0, -1):
            one(15 - pair, pair)
            one(pair, pair)
        one(15, 0)

    def cols_z_wait(pair, count):
        slots = recv_z.at[pl.ds(0, count)]
        copy(6, (on_z(1)[0], 0), lambda i: slots, slots, 14 + pair).wait_recv()

    def cols_z_sent():
        slots = recv_z.at[pl.ds(0, ZN - 1)]
        copy(6, (on_z(1)[0], 0), lambda i: slots, slots, 14).wait_send()

    barrier = pltpu.get_barrier_semaphore()
    orb_in.start()
    ztab_in.start()

    for d in FAR_FIRST[ZN]:
        pl.semaphore_signal(barrier, inc=1, device_id=on_z(d)[0], device_id_type=MESH)
    for d in FAR_FIRST[peers]:
        pl.semaphore_signal(barrier, inc=1, device_id=on_plane(d)[0], device_id_type=MESH)

    for load in loads[2:]:
        load.start()

    used = count_ref[block]
    row32 = lax.broadcasted_iota(jnp.int32, (32, GRID), 0)
    active = jnp.where(band * 4 + row32 % 4 < used, 1.0, 0.0).astype(F32)
    orb_in.wait()
    for n in range(8):
        for c in range(2):
            piece = orb_ref[2 * n + c].astype(F32)
            wide[0, 32 * c + 4 * n : 32 * c + 4 * n + 4, :] = piece[:, 0:128]
            wide[1, 32 * c + 4 * n : 32 * c + 4 * n + 4, 0:64] = piece[:, 128:192]

    def wide_rows(rows):
        return jnp.concatenate([wide[h, rows, :] for h in range(2)], axis=1)[:, 0:GRID]

    real = wide_rows(slice(0, 32)) * active
    imag = wide_rows(slice(32, 64)) * active
    for start, part in ((0, real), (32, imag), (64, -real)):
        wide[0, start : start + 32, :] = part[:, 0:128]
        wide[1, start : start + 32, 0:64] = part[:, 128:192]
    real = real.astype(BF16)
    imag = imag.astype(BF16)
    ztab_in.wait()
    along_z = (
        dot(real, ztab_ref[0:192, :])
        + dot(real, ztab_ref[384:576, :])
        + dot(imag, ztab_ref[192:384, :])
        + dot(imag, ztab_ref[576:768, :])
    )
    for x in range(XN):
        for n in range(8):
            send_b[8 * x + n] = along_z[4 * n : 4 * n + 4, 128 * x : 128 * x + 128].astype(BF16)

    def slot_rows(slot, starts):
        parts = [wide_rows(pl.ds(start + slot, 8, stride=4)) for start in starts]
        return jnp.concatenate(parts, axis=0).astype(BF16)

    proj_in.wait()
    partial = jnp.zeros((16, 512), F32)
    for slot in range(4):
        partial += dot(slot_rows(slot, (0, 32)), proj_ref[slot * 192 : (slot + 1) * 192, :])
        partial += dot(slot_rows(slot, (32, 64)), proj_ref[(slot + 4) * 192 : (slot + 5) * 192, :])
    for x in range(XN):
        for c in range(2):
            send_pb[8 * x : 8 * x + 8, c, :] = partial[8 * c : 8 * c + 8, 128 * x : 128 * x + 128]

    pl.semaphore_wait(barrier, ZN + peers - 2)
    cols_b[0]()
    proj_b[0]()

    stage[...] = jnp.zeros_like(stage)
    found[...] = jnp.zeros_like(found)
    grid_sum[...] = jnp.zeros_like(grid_sum)
    site_in.wait()

    def sources(t):
        return lax.rem(zz + ZN - t, ZN), lax.rem(zz + t + 1, ZN)

    rows = lax.broadcasted_iota(jnp.int32, (GRID, 128), 0)
    is_even = rows < 97
    frequency = jnp.where(is_even, rows, rows - 96)

    def folded(position):
        distance = jnp.minimum(position, GRID - position)
        sign = jnp.where(position < 96, 1.0, -1.0).astype(F32)
        return jnp.where(frequency == distance, jnp.where(is_even, 1.0, sign), 0.0).astype(BF16)

    @pl.loop(0, 8)
    def _(t):
        for h, s in enumerate(sources(t)):
            site = site_ref[pl.ds(s, 1), :]
            kx = (site * 43691) >> 23
            lanes = pl.ds(pl.multiple_of(t * 256 + h * 128, 128), 128)
            picks_x[:, lanes] = folded(kx)
            picks_y[:, lanes] = folded(site - kx * 192)

    recv_b[pl.ds(me, 1)] = send_b[pl.ds(me, 1)]
    cols_b[1]()
    for p in range(peers):
        turn[4 * p : 4 * p + 4, :] = recv_b[p].astype(F32)
    turned = turn[...].T
    for c in range(2):
        for zi in range(3):
            stage[pl.ds(c * 3 + zi, 16, stride=8), :] = turned[64 * c + 16 * zi : 64 * c + 16 * zi + 16]
    send_z[...] = stage[...].reshape(16, 8, 128).astype(BF16)
    cols_z_start()
    recv_z[pl.ds(zz, 1)] = send_z[pl.ds(zz, 1)]

    recv_pb[pl.ds(me, 1)] = send_pb[pl.ds(me, 1)]
    proj_b[1]()
    total = recv_pb[0]
    for p in range(1, peers):
        total += recv_pb[p]
    send_pz[...] = total
    recv_pz[pl.ds(zz, 1)] = total[None]
    proj_z[0]()

    atom_in.wait()
    coup_in.wait()
    atoms = lax.broadcasted_iota(jnp.int32, (64, 128), 0)
    marks = jnp.concatenate(
        [jnp.where(atoms == atom_ref[q : q + 1, :], 1.0, 0.0).astype(F32) for q in range(4)], axis=1
    )
    same = dot(marks.T.astype(BF16), marks.astype(BF16))
    coupled = jnp.where(same > 0.5, coup_ref[...], 0.0)
    part_h, part_l = split(coupled)
    coupled_h[...] = part_h
    coupled_l[...] = part_l

    def scatter(t):
        for h, s in enumerate(sources(t)):
            arrived = recv_z[s].astype(F32)
            spots = picks_x[:, pl.ds(pl.multiple_of(t * 256 + h * 128, 128), 128)]
            for i in range(6):
                row = (i % 2) * 3 + i // 2
                value = arrived[row : row + 1]
                spread = jnp.broadcast_to(value, (GRID, 128)).astype(BF16)
                weights[i * 192 : (i + 1) * 192, h * 128 : (h + 1) * 128] = spots * spread
        grid_sum[...] += dot_nt(weights[...], picks_y[:, pl.ds(pl.multiple_of(t * 256, 256), 256)])

    cols_z_wait(0, 1)
    scatter(0)

    @pl.loop(1, 8)
    def _(t):
        cols_z_wait(t, 2)
        scatter(t)

    cols_z_sent()

    plane_in.wait()
    pot_in.wait()
    across_h = plane_ref[0:192, :]
    across_l = plane_ref[192:384, :]
    down_h = plane_ref[384:576, :]
    down_l = plane_ref[576:768, :]
    scale = 1.0 / float(GRID**3)
    even_row = lax.broadcasted_iota(jnp.int32, (GRID, GRID), 0) < 97
    even_lane = lax.broadcasted_iota(jnp.int32, (GRID, GRID), 1) < 97

    def times_i(even, real, imag):
        return jnp.where(even, real, -imag), jnp.where(even, imag, real)

    def times_minus_i(even, real, imag):
        return jnp.where(even, real, imag), jnp.where(even, imag, -real)

    def from_left(first, value):
        high, low = split(value)
        both = dot(plane_ref[first : first + 384, :], high)
        return both[0:192] + both[192:384] + dot(plane_ref[first : first + 192, :], low)

    def from_right(real, imag, table_h, table_l):
        high, low = split(jnp.concatenate([real, imag], axis=0))
        both = dot(high, table_h) + dot(high, table_l) + dot(low, table_h)
        return both[0:192], both[192:384]

    def one_plane(zi):
        rows = pl.ds(pl.multiple_of(zi * 384, 384), 384)
        start = grid_sum[rows, :]
        real, imag = times_i(even_lane, start[0:192], start[192:384])
        real, imag = from_right(real, imag, down_h, down_l)
        real, imag = times_i(even_row, real, imag)
        field = pot_ref[zi] * scale
        real = from_left(0, real) * field
        imag = from_left(0, imag) * field
        real = from_left(384, real)
        imag = from_left(384, imag)
        real, imag = times_minus_i(even_row, real, imag)
        real, imag = from_right(real, imag, across_h, across_l)
        real, imag = times_minus_i(even_lane, real, imag)
        grid_back[rows, :] = jnp.concatenate([real, imag], axis=0).astype(BF16)

    one_plane(0)

    proj_z[1]()
    total = recv_pz[0]
    for z in range(1, ZN):
        total += recv_pz[z]
    back_pb[...] = total
    got_pb[pl.ds(me, 1)] = total[None]
    sums_b[0]()

    @pl.loop(1, 3)
    def _(zi):
        one_plane(zi)

    def gather(t):
        lanes = pl.ds(pl.multiple_of(t * 256, 256), 256)
        picked = dot(grid_back[...], picks_y[:, lanes])
        spots = picks_x[:, lanes].astype(F32)
        for i in range(6):
            value = jnp.sum(picked[i * 192 : (i + 1) * 192] * spots, axis=0, keepdims=True)
            for h in range(2):
                row = h * 8 + (i % 2) * 3 + i // 2
                found[row : row + 1, :] = value[:, h * 128 : (h + 1) * 128]
        for h, s in enumerate(sources(t)):
            back_z[s] = found[8 * h : 8 * h + 8, :]

    @pl.loop(0, 7)
    def _(i):
        t = 7 - i
        gather(t)
        home_z[2](t + 1)
        home_z[2](16 - t)

    gather(0)
    home_z[2](1)
    got_z[pl.ds(zz, 1)] = back_z[pl.ds(zz, 1)]

    sums_b[1]()
    pairs = []
    for part in range(4):
        real = got_pb[8 * part : 8 * part + 8, 0, :]
        imag = got_pb[8 * part : 8 * part + 8, 1, :]
        pairs.append(jnp.concatenate([real, imag, -imag, real], axis=0))
    high, low = split(jnp.concatenate(pairs, axis=1))
    weighted = dot_nt(high, coupled_h[...]) + dot_nt(high, coupled_l[...]) + dot_nt(low, coupled_h[...])
    weighted = weighted.astype(BF16)
    for slot in range(4):
        mixed = dot_nt(weighted[0:16], proj_ref[slot * 192 : (slot + 1) * 192, :]) + dot_nt(
            weighted[16:32], proj_ref[(slot + 4) * 192 : (slot + 5) * 192, :]
        )
        mixed = jnp.concatenate([mixed, jnp.zeros((16, 64), F32)], axis=1)
        for c in range(2):
            for h in range(2):
                wide[h, pl.ds(32 * c + slot, 8, stride=4), :] = mixed[8 * c : 8 * c + 8, 128 * h : 128 * h + 128]

    home_z[1]()
    stage[...] = got_z[...].reshape(128, 128)
    rows = []
    for c in range(2):
        rows += [stage[pl.ds(c * 3 + zi, 16, stride=8), :] for zi in range(3)]
        rows.append(jnp.zeros((16, 128), F32))
    turned = jnp.concatenate(rows, axis=0).T
    for p in range(peers):
        back_b[p] = turned[4 * p : 4 * p + 4]
    home_b[0]()
    got_b[pl.ds(me, 1)] = back_b[pl.ds(me, 1)]
    home_b[1]()
    for x in range(XN):
        for n in range(8):
            turn[32 * x + 4 * n : 32 * x + 4 * n + 4, :] = got_b[8 * x + n]
    wave = jnp.concatenate([turn[32 * x : 32 * x + 32, :] for x in range(XN)], axis=1)
    high, low = split(wave)
    for c in range(2):
        table_h = ztab_ref[192 * c : 192 * c + 192, :]
        local = dot_nt(high, table_h) + dot_nt(high, ztab_ref[192 * c + 384 : 192 * c + 576, :]) + dot_nt(low, table_h)
        result = (local + wide_rows(slice(32 * c, 32 * c + 32))) * active
        for n in range(8):
            out_ref[2 * n + c] = result[4 * n : 4 * n + 4, :]


def on_device(orbitals, projectors, potential, couplings, atom_index, column_site, column_count):
    plane, ztab = (jnp.asarray(t) for t in make_tables())
    vmem = pl.BlockSpec(memory_space=pltpu.VMEM)
    hbm = pl.BlockSpec(memory_space=pltpu.HBM)
    smem = pl.BlockSpec(memory_space=pltpu.SMEM)
    flat = projectors.transpose(1, 2, 3, 0).reshape(8 * GRID, 512)
    scratch = lambda *shape: pltpu.VMEM(shape, F32)
    out = pl.pallas_call(
        kernel,
        out_shape=pltpu.VMEM((16, 4, GRID), F32),
        in_specs=[smem] + [hbm] * 8,
        out_specs=vmem,
        scratch_shapes=[
            pltpu.VMEM((16, 128), jnp.int32),
            pltpu.VMEM((4, 128), jnp.int32),
            pltpu.VMEM((16, 4, GRID), BF16),
            pltpu.VMEM((8 * GRID, 512), BF16),
            scratch(3, GRID, GRID),
            scratch(512, 512),
            pltpu.VMEM((768, GRID), BF16),
            pltpu.VMEM((768, 512), BF16),
            scratch(2, 128, 128),
            pltpu.VMEM((32, 4, 128), BF16),
            pltpu.VMEM((32, 4, 128), BF16),
            scratch(32, 2, 128),
            scratch(32, 2, 128),
            scratch(128, 128),
            scratch(128, 128),
            pltpu.VMEM((16, 8, 128), BF16),
            pltpu.VMEM((16, 8, 128), BF16),
            scratch(2, 128),
            scratch(16, 2, 128),
            pltpu.VMEM((GRID, 2048), BF16),
            pltpu.VMEM((GRID, 2048), BF16),
            pltpu.VMEM((1152, 256), BF16),
            scratch(1152, GRID),
            pltpu.VMEM((1152, GRID), BF16),
            pltpu.VMEM((512, 512), BF16),
            pltpu.VMEM((512, 512), BF16),
            scratch(16, 128),
            scratch(16, 8, 128),
            scratch(16, 8, 128),
            scratch(32, 4, 128),
            scratch(32, 4, 128),
            scratch(2, 128),
            scratch(32, 2, 128),
            pltpu.SemaphoreType.DMA((22,)),
            pltpu.SemaphoreType.DMA((8,)),
        ],
        compiler_params=pltpu.CompilerParams(
            collective_id=0, has_side_effects=True, vmem_limit_bytes=60000000
        ),
    )(
        column_count,
        column_site.reshape(16, 128),
        atom_index.reshape(4, 128),
        orbitals.reshape(16, 4, GRID),
        flat,
        potential,
        couplings,
        plane,
        ztab,
    )
    return out.reshape(8, 2, 4, GRID)


def solution(mesh):
    return jax.shard_map(
        on_device,
        mesh=mesh,
        in_specs=(
            P(None, None, ("ga", "band"), None),
            P(None, None, ("ga", "band"), None),
            P("ga", None, None),
            P(),
            P(),
            P(),
            P(),
        ),
        out_specs=P(None, None, ("ga", "band"), None),
        check_vma=False,
    )
```

```python
import math

import jax
import jax.numpy as jnp
import ml_dtypes
import numpy as np
from jax import lax
from jax.experimental import pallas as pl
from jax.experimental.pallas import tpu as pltpu
from jax.sharding import PartitionSpec as P

MESH = pl.DeviceIdType.MESH
F32 = jnp.float32
BF16 = jnp.bfloat16
GRID = 192
ZN, XN, BN = 16, 4, 8
FAR_FIRST = {
    ZN: [8, 9, 7, 10, 6, 11, 5, 12, 4, 13, 3, 14, 2, 15, 1],
    XN * BN: [d % 32 for d in range(20, 52) if d != 32],
}


def split_host(table):
    high = table.astype(ml_dtypes.bfloat16)
    low = (table - high.astype(np.float64)).astype(ml_dtypes.bfloat16)
    return high, low


def make_tables():
    points = np.arange(GRID)
    phases = (points[:, None] * points[None, :] % GRID) * (2.0 * math.pi / GRID)
    down = np.concatenate([np.cos(phases[0:97]), np.sin(phases[1:96])], axis=0)
    plane = np.concatenate(split_host(np.ascontiguousarray(down.T)) + split_host(down), axis=0)
    from_real = np.zeros((GRID, XN, 2, 64))
    from_imag = np.zeros((GRID, XN, 2, 64))
    for x in range(XN):
        for sub in range(3):
            angles = phases[:, 12 * np.arange(ZN) + 3 * x + sub]
            lanes = slice(16 * sub, 16 * sub + 16)
            from_real[:, x, 0, lanes] = np.cos(angles)
            from_real[:, x, 1, lanes] = np.sin(angles)
            from_imag[:, x, 0, lanes] = -np.sin(angles)
            from_imag[:, x, 1, lanes] = np.cos(angles)
    real_h, real_l = split_host(from_real.reshape(GRID, 512))
    imag_h, imag_l = split_host(from_imag.reshape(GRID, 512))
    return plane, np.concatenate([real_h, imag_h, real_l, imag_l], axis=0)


def dot(left, right):
    return lax.dot_general(left, right, (((1,), (0,)), ((), ())), preferred_element_type=F32)


def dot_nt(left, right):
    return lax.dot_general(left, right, (((1,), (1,)), ((), ())), preferred_element_type=F32)


def split(value):
    high = value.astype(BF16)
    return high, (value - high.astype(F32)).astype(BF16)


def kernel(
    count_ref, site_hbm, atom_hbm, orb_hbm, proj_hbm, pot_hbm, coup_hbm, plane_hbm, ztab_hbm, out_ref,
    site_ref, atom_ref, orb_ref, proj_ref, pot_ref, coup_ref, plane_ref, ztab_ref,
    wide, send_b, recv_b, send_pb, recv_pb, turn, stage, send_z, recv_z, send_pz, recv_pz,
    picks_x, picks_y, weights, grid_sum, grid_back, coupled_h, coupled_l, found, back_z, got_z,
    back_b, got_b, back_pb, got_pb, sems, load_sems, relays,
):
    block = lax.axis_index("ga")
    band = lax.axis_index("band")
    zz = lax.div(block, XN)
    xx = lax.rem(block, XN)
    me = xx * BN + band

    arrays = (
        (orb_hbm, orb_ref), (ztab_hbm, ztab_ref), (proj_hbm, proj_ref), (site_hbm, site_ref),
        (atom_hbm, atom_ref), (coup_hbm, coup_ref), (plane_hbm, plane_ref), (pot_hbm, pot_ref),
    )
    loads = [pltpu.make_async_copy(far, near, load_sems.at[i]) for i, (far, near) in enumerate(arrays)]
    orb_in, ztab_in, proj_in, site_in, atom_in, coup_in, plane_in, pot_in = loads

    def on_plane(d):
        index = lax.rem(me + d, XN * BN)
        return (zz * XN + lax.div(index, BN), lax.rem(index, BN)), index

    def on_z(d):
        index = lax.rem(zz + d, ZN)
        return (index * XN + xx, band), index

    peers = XN * BN

    def copy(number, target_of, source, target, arrival=None):
        device, index = target_of
        return pltpu.make_async_remote_copy(
            src_ref=source(index),
            dst_ref=target,
            send_sem=sems.at[2 * number],
            recv_sem=sems.at[2 * number + 1 if arrival is None else arrival],
            device_id=device,
            device_id_type=MESH,
        )

    def exchange(number, size, where, source, target, slots):
        def start_one(d):
            copy(number, where(d), source, target).start()

        def start():
            for d in FAR_FIRST[size]:
                start_one(d)

        def wait():
            every = copy(number, (where(1)[0], 0), lambda i: slots, slots)
            every.wait_send()
            every.wait_recv()

        return start, wait, start_one

    cols_b = exchange(0, peers, on_plane, lambda i: send_b.at[i], recv_b.at[me], recv_b.at[pl.ds(0, peers - 1)])
    proj_b = exchange(1, peers, on_plane, lambda i: send_pb.at[i], recv_pb.at[me], recv_pb.at[pl.ds(0, peers - 1)])
    proj_z = exchange(2, ZN, on_z, lambda i: send_pz, recv_pz.at[zz], recv_pz.at[pl.ds(0, ZN - 1)])
    sums_b = exchange(3, peers, on_plane, lambda i: back_pb, got_pb.at[me], got_pb.at[pl.ds(0, peers - 1)])
    home_z = exchange(4, ZN, on_z, lambda i: back_z.at[i], got_z.at[zz], got_z.at[pl.ds(0, ZN - 1)])
    home_b = exchange(5, peers, on_plane, lambda i: back_b.at[i], got_b.at[me], got_b.at[pl.ds(0, peers - 1)])

    def cols_z_start():
        def one(d, pair):
            copy(6, on_z(d), lambda i: send_z.at[i], recv_z.at[zz], 14 + pair).start()

        for pair in range(7, 0, -1):
            one(15 - pair, pair)
            one(pair, pair)
        one(15, 0)

    def cols_z_wait(pair, count):
        slots = recv_z.at[pl.ds(0, count)]
        copy(6, (on_z(1)[0], 0), lambda i: slots, slots, 14 + pair).wait_recv()

    def cols_z_sent():
        slots = recv_z.at[pl.ds(0, ZN - 1)]
        copy(6, (on_z(1)[0], 0), lambda i: slots, slots, 14).wait_send()

    barrier = pltpu.get_barrier_semaphore()
    orb_in.start()
    ztab_in.start()

    for d in FAR_FIRST[peers]:
        pl.semaphore_signal(barrier, inc=1, device_id=on_plane(d)[0], device_id_type=MESH)
    for d in (1, ZN - 1):
        pl.semaphore_signal(barrier, inc=1, device_id=on_z(d)[0], device_id_type=MESH)

    def relay(k):
        for side, d in enumerate((1, ZN - 1)):
            pl.semaphore_signal(relays.at[2 * k + side], inc=1, device_id=on_z(d)[0], device_id_type=MESH)

    def relayed(k):
        for side in range(2):
            pl.semaphore_wait(relays.at[2 * k + side], 1)


    for load in loads[2:]:
        load.start()

    used = count_ref[block]
    row32 = lax.broadcasted_iota(jnp.int32, (32, GRID), 0)
    active = jnp.where(band * 4 + row32 % 4 < used, 1.0, 0.0).astype(F32)
    orb_in.wait()
    for n in range(8):
        for c in range(2):
            piece = orb_ref[2 * n + c].astype(F32)
            wide[0, 32 * c + 4 * n : 32 * c + 4 * n + 4, :] = piece[:, 0:128]
            wide[1, 32 * c + 4 * n : 32 * c + 4 * n + 4, 0:64] = piece[:, 128:192]

    def wide_rows(rows):
        return jnp.concatenate([wide[h, rows, :] for h in range(2)], axis=1)[:, 0:GRID]

    real = wide_rows(slice(0, 32)) * active
    imag = wide_rows(slice(32, 64)) * active
    for start, part in ((0, real), (32, imag), (64, -real)):
        wide[0, start : start + 32, :] = part[:, 0:128]
        wide[1, start : start + 32, 0:64] = part[:, 128:192]
    real = real.astype(BF16)
    imag = imag.astype(BF16)
    ztab_in.wait()
    along_z = (
        dot(real, ztab_ref[0:192, :])
        + dot(real, ztab_ref[384:576, :])
        + dot(imag, ztab_ref[192:384, :])
        + dot(imag, ztab_ref[576:768, :])
    )
    for x in range(XN):
        for n in range(8):
            send_b[8 * x + n] = along_z[4 * n : 4 * n + 4, 128 * x : 128 * x + 128].astype(BF16)

    pl.semaphore_wait(barrier, peers + 1)
    cols_b[0]()
    relay(0)

    def slot_rows(slot, starts):
        parts = [wide_rows(pl.ds(start + slot, 8, stride=4)) for start in starts]
        return jnp.concatenate(parts, axis=0).astype(BF16)

    proj_in.wait()
    partial = jnp.zeros((16, 512), F32)
    for slot in range(4):
        partial += dot(slot_rows(slot, (0, 32)), proj_ref[slot * 192 : (slot + 1) * 192, :])
        partial += dot(slot_rows(slot, (32, 64)), proj_ref[(slot + 4) * 192 : (slot + 5) * 192, :])
    for x in range(XN):
        for c in range(2):
            send_pb[8 * x : 8 * x + 8, c, :] = partial[8 * c : 8 * c + 8, 128 * x : 128 * x + 128]
    proj_b[0]()
    relayed(0)
    relay(1)

    stage[...] = jnp.zeros_like(stage)
    found[...] = jnp.zeros_like(found)
    grid_sum[...] = jnp.zeros_like(grid_sum)
    site_in.wait()

    def sources(t):
        return lax.rem(zz + ZN - t, ZN), lax.rem(zz + t + 1, ZN)

    rows = lax.broadcasted_iota(jnp.int32, (GRID, 128), 0)
    is_even = rows < 97
    frequency = jnp.where(is_even, rows, rows - 96)

    def folded(position):
        distance = jnp.minimum(position, GRID - position)
        sign = jnp.where(position < 96, 1.0, -1.0).astype(F32)
        return jnp.where(frequency == distance, jnp.where(is_even, 1.0, sign), 0.0).astype(BF16)

    def pick(t):
        for h, s in enumerate(sources(t)):
            site = site_ref[pl.ds(s, 1), :]
            kx = (site * 43691) >> 23
            lanes = pl.ds(pl.multiple_of(t * 256 + h * 128, 128), 128)
            picks_x[:, lanes] = folded(kx)
            picks_y[:, lanes] = folded(site - kx * 192)

    pick(0)
    pick(1)
    relayed(1)
    for k in range(2, 7):
        relay(k)
        pick(k)
        if k == 2:
            pick(7)
        relayed(k)

    recv_b[pl.ds(me, 1)] = send_b[pl.ds(me, 1)]
    cols_b[1]()
    for p in range(peers):
        turn[4 * p : 4 * p + 4, :] = recv_b[p].astype(F32)
    turned = turn[...].T
    for c in range(2):
        for zi in range(3):
            stage[pl.ds(c * 3 + zi, 16, stride=8), :] = turned[64 * c + 16 * zi : 64 * c + 16 * zi + 16]
    send_z[...] = stage[...].reshape(16, 8, 128).astype(BF16)
    cols_z_start()
    recv_z[pl.ds(zz, 1)] = send_z[pl.ds(zz, 1)]

    recv_pb[pl.ds(me, 1)] = send_pb[pl.ds(me, 1)]
    proj_b[1]()
    total = recv_pb[0]
    for p in range(1, peers):
        total += recv_pb[p]
    send_pz[...] = total
    recv_pz[pl.ds(zz, 1)] = total[None]
    proj_z[0]()

    atom_in.wait()
    coup_in.wait()
    atoms = lax.broadcasted_iota(jnp.int32, (64, 128), 0)
    marks = jnp.concatenate(
        [jnp.where(atoms == atom_ref[q : q + 1, :], 1.0, 0.0).astype(F32) for q in range(4)], axis=1
    )
    same = dot(marks.T.astype(BF16), marks.astype(BF16))
    coupled = jnp.where(same > 0.5, coup_ref[...], 0.0)
    part_h, part_l = split(coupled)
    coupled_h[...] = part_h
    coupled_l[...] = part_l

    def scatter(t):
        for h, s in enumerate(sources(t)):
            arrived = recv_z[s].astype(F32)
            spots = picks_x[:, pl.ds(pl.multiple_of(t * 256 + h * 128, 128), 128)]
            for i in range(6):
                row = (i % 2) * 3 + i // 2
                value = arrived[row : row + 1]
                spread = jnp.broadcast_to(value, (GRID, 128)).astype(BF16)
                weights[i * 192 : (i + 1) * 192, h * 128 : (h + 1) * 128] = spots * spread
        grid_sum[...] += dot_nt(weights[...], picks_y[:, pl.ds(pl.multiple_of(t * 256, 256), 256)])

    cols_z_wait(0, 1)
    scatter(0)

    @pl.loop(1, 8)
    def _(t):
        cols_z_wait(t, 2)
        scatter(t)

    cols_z_sent()

    plane_in.wait()
    pot_in.wait()
    across_h = plane_ref[0:192, :]
    across_l = plane_ref[192:384, :]
    down_h = plane_ref[384:576, :]
    down_l = plane_ref[576:768, :]
    scale = 1.0 / float(GRID**3)
    even_row = lax.broadcasted_iota(jnp.int32, (GRID, GRID), 0) < 97
    even_lane = lax.broadcasted_iota(jnp.int32, (GRID, GRID), 1) < 97

    def times_i(even, real, imag):
        return jnp.where(even, real, -imag), jnp.where(even, imag, real)

    def times_minus_i(even, real, imag):
        return jnp.where(even, real, imag), jnp.where(even, imag, -real)

    def from_left(first, value):
        high, low = split(value)
        both = dot(plane_ref[first : first + 384, :], high)
        return both[0:192] + both[192:384] + dot(plane_ref[first : first + 192, :], low)

    def from_right(real, imag, table_h, table_l):
        high, low = split(jnp.concatenate([real, imag], axis=0))
        both = dot(high, table_h) + dot(high, table_l) + dot(low, table_h)
        return both[0:192], both[192:384]

    def one_plane(zi):
        rows = pl.ds(pl.multiple_of(zi * 384, 384), 384)
        start = grid_sum[rows, :]
        real, imag = times_i(even_lane, start[0:192], start[192:384])
        real, imag = from_right(real, imag, down_h, down_l)
        real, imag = times_i(even_row, real, imag)
        field = pot_ref[zi] * scale
        real = from_left(0, real) * field
        imag = from_left(0, imag) * field
        real = from_left(384, real)
        imag = from_left(384, imag)
        real, imag = times_minus_i(even_row, real, imag)
        real, imag = from_right(real, imag, across_h, across_l)
        real, imag = times_minus_i(even_lane, real, imag)
        grid_back[rows, :] = jnp.concatenate([real, imag], axis=0).astype(BF16)

    one_plane(0)

    proj_z[1]()
    total = recv_pz[0]
    for z in range(1, ZN):
        total += recv_pz[z]
    back_pb[...] = total
    got_pb[pl.ds(me, 1)] = total[None]
    sums_b[0]()

    @pl.loop(1, 3)
    def _(zi):
        one_plane(zi)

    def gather(t):
        lanes = pl.ds(pl.multiple_of(t * 256, 256), 256)
        picked = dot(grid_back[...], picks_y[:, lanes])
        spots = picks_x[:, lanes].astype(F32)
        for i in range(6):
            value = jnp.sum(picked[i * 192 : (i + 1) * 192] * spots, axis=0, keepdims=True)
            for h in range(2):
                row = h * 8 + (i % 2) * 3 + i // 2
                found[row : row + 1, :] = value[:, h * 128 : (h + 1) * 128]
        for h, s in enumerate(sources(t)):
            back_z[s] = found[8 * h : 8 * h + 8, :]

    @pl.loop(0, 7)
    def _(i):
        t = 7 - i
        gather(t)
        home_z[2](t + 1)
        home_z[2](16 - t)

    gather(0)
    home_z[2](1)
    got_z[pl.ds(zz, 1)] = back_z[pl.ds(zz, 1)]

    sums_b[1]()
    pairs = []
    for part in range(4):
        real = got_pb[8 * part : 8 * part + 8, 0, :]
        imag = got_pb[8 * part : 8 * part + 8, 1, :]
        pairs.append(jnp.concatenate([real, imag, -imag, real], axis=0))
    high, low = split(jnp.concatenate(pairs, axis=1))
    weighted = dot_nt(high, coupled_h[...]) + dot_nt(high, coupled_l[...]) + dot_nt(low, coupled_h[...])
    weighted = weighted.astype(BF16)
    for slot in range(4):
        mixed = dot_nt(weighted[0:16], proj_ref[slot * 192 : (slot + 1) * 192, :]) + dot_nt(
            weighted[16:32], proj_ref[(slot + 4) * 192 : (slot + 5) * 192, :]
        )
        mixed = jnp.concatenate([mixed, jnp.zeros((16, 64), F32)], axis=1)
        for c in range(2):
            for h in range(2):
                wide[h, pl.ds(32 * c + slot, 8, stride=4), :] = mixed[8 * c : 8 * c + 8, 128 * h : 128 * h + 128]

    home_z[1]()
    stage[...] = got_z[...].reshape(128, 128)
    rows = []
    for c in range(2):
        rows += [stage[pl.ds(c * 3 + zi, 16, stride=8), :] for zi in range(3)]
        rows.append(jnp.zeros((16, 128), F32))
    turned = jnp.concatenate(rows, axis=0).T
    for p in range(peers):
        back_b[p] = turned[4 * p : 4 * p + 4]
    home_b[0]()
    got_b[pl.ds(me, 1)] = back_b[pl.ds(me, 1)]
    home_b[1]()
    for x in range(XN):
        for n in range(8):
            turn[32 * x + 4 * n : 32 * x + 4 * n + 4, :] = got_b[8 * x + n]
    wave = jnp.concatenate([turn[32 * x : 32 * x + 32, :] for x in range(XN)], axis=1)
    high, low = split(wave)
    for c in range(2):
        table_h = ztab_ref[192 * c : 192 * c + 192, :]
        local = dot_nt(high, table_h) + dot_nt(high, ztab_ref[192 * c + 384 : 192 * c + 576, :]) + dot_nt(low, table_h)
        result = (local + wide_rows(slice(32 * c, 32 * c + 32))) * active
        for n in range(8):
            out_ref[2 * n + c] = result[4 * n : 4 * n + 4, :]


def on_device(orbitals, projectors, potential, couplings, atom_index, column_site, column_count):
    plane, ztab = (jnp.asarray(t) for t in make_tables())
    vmem = pl.BlockSpec(memory_space=pltpu.VMEM)
    hbm = pl.BlockSpec(memory_space=pltpu.HBM)
    smem = pl.BlockSpec(memory_space=pltpu.SMEM)
    flat = projectors.transpose(1, 2, 3, 0).reshape(8 * GRID, 512)
    scratch = lambda *shape: pltpu.VMEM(shape, F32)
    out = pl.pallas_call(
        kernel,
        out_shape=pltpu.VMEM((16, 4, GRID), F32),
        in_specs=[smem] + [hbm] * 8,
        out_specs=vmem,
        scratch_shapes=[
            pltpu.VMEM((16, 128), jnp.int32),
            pltpu.VMEM((4, 128), jnp.int32),
            pltpu.VMEM((16, 4, GRID), BF16),
            pltpu.VMEM((8 * GRID, 512), BF16),
            scratch(3, GRID, GRID),
            scratch(512, 512),
            pltpu.VMEM((768, GRID), BF16),
            pltpu.VMEM((768, 512), BF16),
            scratch(2, 128, 128),
            pltpu.VMEM((32, 4, 128), BF16),
            pltpu.VMEM((32, 4, 128), BF16),
            scratch(32, 2, 128),
            scratch(32, 2, 128),
            scratch(128, 128),
            scratch(128, 128),
            pltpu.VMEM((16, 8, 128), BF16),
            pltpu.VMEM((16, 8, 128), BF16),
            scratch(2, 128),
            scratch(16, 2, 128),
            pltpu.VMEM((GRID, 2048), BF16),
            pltpu.VMEM((GRID, 2048), BF16),
            pltpu.VMEM((1152, 256), BF16),
            scratch(1152, GRID),
            pltpu.VMEM((1152, GRID), BF16),
            pltpu.VMEM((512, 512), BF16),
            pltpu.VMEM((512, 512), BF16),
            scratch(16, 128),
            scratch(16, 8, 128),
            scratch(16, 8, 128),
            scratch(32, 4, 128),
            scratch(32, 4, 128),
            scratch(2, 128),
            scratch(32, 2, 128),
            pltpu.SemaphoreType.DMA((22,)),
            pltpu.SemaphoreType.DMA((8,)),
            pltpu.SemaphoreType.REGULAR((14,)),
        ],
        compiler_params=pltpu.CompilerParams(
            collective_id=0, has_side_effects=True, vmem_limit_bytes=60000000
        ),
    )(
        column_count,
        column_site.reshape(16, 128),
        atom_index.reshape(4, 128),
        orbitals.reshape(16, 4, GRID),
        flat,
        potential,
        couplings,
        plane,
        ztab,
    )
    return out.reshape(8, 2, 4, GRID)


def solution(mesh):
    return jax.shard_map(
        on_device,
        mesh=mesh,
        in_specs=(
            P(None, None, ("ga", "band"), None),
            P(None, None, ("ga", "band"), None),
            P("ga", None, None),
            P(),
            P(),
            P(),
            P(),
        ),
        out_specs=P(None, None, ("ga", "band"), None),
        check_vma=False,
    )
```

```python
import math

import jax
import jax.numpy as jnp
import ml_dtypes
import numpy as np
from jax import lax
from jax.experimental import pallas as pl
from jax.experimental.pallas import tpu as pltpu
from jax.sharding import PartitionSpec as P

MESH = pl.DeviceIdType.MESH
F32 = jnp.float32
BF16 = jnp.bfloat16
GRID = 192
ZN, XN, BN = 16, 4, 8
FAR_FIRST = {
    ZN: [8, 9, 7, 10, 6, 11, 5, 12, 4, 13, 3, 14, 2, 15, 1],
    XN * BN: [d % 32 for d in range(20, 52) if d != 32],
}


def split_host(table):
    high = table.astype(ml_dtypes.bfloat16)
    low = (table - high.astype(np.float64)).astype(ml_dtypes.bfloat16)
    return high, low


def make_tables():
    points = np.arange(GRID)
    phases = (points[:, None] * points[None, :] % GRID) * (2.0 * math.pi / GRID)
    down = np.concatenate([np.cos(phases[0:97]), np.sin(phases[1:96])], axis=0)
    plane = np.concatenate(split_host(np.ascontiguousarray(down.T)) + split_host(down), axis=0)
    from_real = np.zeros((GRID, XN, 2, 64))
    from_imag = np.zeros((GRID, XN, 2, 64))
    for x in range(XN):
        for sub in range(3):
            angles = phases[:, 12 * np.arange(ZN) + 3 * x + sub]
            lanes = slice(16 * sub, 16 * sub + 16)
            from_real[:, x, 0, lanes] = np.cos(angles)
            from_real[:, x, 1, lanes] = np.sin(angles)
            from_imag[:, x, 0, lanes] = -np.sin(angles)
            from_imag[:, x, 1, lanes] = np.cos(angles)
    real_h, real_l = split_host(from_real.reshape(GRID, 512))
    imag_h, imag_l = split_host(from_imag.reshape(GRID, 512))
    return plane, np.concatenate([real_h, imag_h, real_l, imag_l], axis=0)


def dot(left, right):
    return lax.dot_general(left, right, (((1,), (0,)), ((), ())), preferred_element_type=F32)


def dot_nt(left, right):
    return lax.dot_general(left, right, (((1,), (1,)), ((), ())), preferred_element_type=F32)


def split(value):
    high = value.astype(BF16)
    return high, (value - high.astype(F32)).astype(BF16)


def kernel(
    count_ref, site_hbm, atom_hbm, orb_hbm, proj_hbm, pot_hbm, coup_hbm, plane_hbm, ztab_hbm, out_ref,
    site_ref, atom_ref, orb_ref, proj_ref, pot_ref, coup_ref, plane_ref, ztab_ref,
    wide, send_b, recv_b, send_pb, recv_pb, turn, stage, send_z, recv_z, send_pz, recv_pz,
    picks_x, picks_y, weights, grid_sum, grid_back, coupled_h, coupled_l, found, back_z, got_z,
    back_b, got_b, back_pb, got_pb, sems, load_sems, relays,
):
    block = lax.axis_index("ga")
    band = lax.axis_index("band")
    zz = lax.div(block, XN)
    xx = lax.rem(block, XN)
    me = xx * BN + band

    arrays = (
        (orb_hbm, orb_ref), (ztab_hbm, ztab_ref), (proj_hbm, proj_ref), (site_hbm, site_ref),
        (atom_hbm, atom_ref), (coup_hbm, coup_ref), (plane_hbm, plane_ref), (pot_hbm, pot_ref),
    )
    loads = [pltpu.make_async_copy(far, near, load_sems.at[i]) for i, (far, near) in enumerate(arrays)]
    orb_in, ztab_in, proj_in, site_in, atom_in, coup_in, plane_in, pot_in = loads

    def on_plane(d):
        index = lax.rem(me + d, XN * BN)
        return (zz * XN + lax.div(index, BN), lax.rem(index, BN)), index

    def on_z(d):
        index = lax.rem(zz + d, ZN)
        return (index * XN + xx, band), index

    peers = XN * BN

    def copy(number, target_of, source, target, arrival=None):
        device, index = target_of
        return pltpu.make_async_remote_copy(
            src_ref=source(index),
            dst_ref=target,
            send_sem=sems.at[2 * number],
            recv_sem=sems.at[2 * number + 1 if arrival is None else arrival],
            device_id=device,
            device_id_type=MESH,
        )

    def exchange(number, size, where, source, target, slots):
        def start_one(d):
            copy(number, where(d), source, target).start()

        def start():
            for d in FAR_FIRST[size]:
                start_one(d)

        def wait():
            every = copy(number, (where(1)[0], 0), lambda i: slots, slots)
            every.wait_send()
            every.wait_recv()

        return start, wait, start_one

    cols_b = exchange(0, peers, on_plane, lambda i: send_b.at[i], recv_b.at[me], recv_b.at[pl.ds(0, peers - 1)])
    proj_b = exchange(1, peers, on_plane, lambda i: send_pb.at[i], recv_pb.at[me], recv_pb.at[pl.ds(0, peers - 1)])
    proj_z = exchange(2, ZN, on_z, lambda i: send_pz, recv_pz.at[zz], recv_pz.at[pl.ds(0, ZN - 1)])
    sums_b = exchange(3, peers, on_plane, lambda i: back_pb, got_pb.at[me], got_pb.at[pl.ds(0, peers - 1)])
    home_z = exchange(4, ZN, on_z, lambda i: back_z.at[i], got_z.at[zz], got_z.at[pl.ds(0, ZN - 1)])
    home_b = exchange(5, peers, on_plane, lambda i: back_b.at[i], got_b.at[me], got_b.at[pl.ds(0, peers - 1)])

    def cols_z_start():
        def one(d, pair):
            copy(6, on_z(d), lambda i: send_z.at[i], recv_z.at[zz], 14 + pair).start()

        for pair in range(7, 0, -1):
            one(15 - pair, pair)
            one(pair, pair)
        one(15, 0)

    def cols_z_wait(pair, count):
        slots = recv_z.at[pl.ds(0, count)]
        copy(6, (on_z(1)[0], 0), lambda i: slots, slots, 14 + pair).wait_recv()

    def cols_z_sent():
        slots = recv_z.at[pl.ds(0, ZN - 1)]
        copy(6, (on_z(1)[0], 0), lambda i: slots, slots, 14).wait_send()

    barrier = pltpu.get_barrier_semaphore()
    orb_in.start()
    ztab_in.start()

    for d in (4, ZN - 4, 3, ZN - 3):
        pl.semaphore_signal(barrier, inc=1, device_id=on_z(d)[0], device_id_type=MESH)
    for d in FAR_FIRST[peers]:
        pl.semaphore_signal(barrier, inc=1, device_id=on_plane(d)[0], device_id_type=MESH)
    for d in (2, ZN - 2, 1, ZN - 1):
        pl.semaphore_signal(barrier, inc=1, device_id=on_z(d)[0], device_id_type=MESH)

    def relay():
        for side, d in enumerate((4, ZN - 4)):
            pl.semaphore_signal(relays.at[side], inc=1, device_id=on_z(d)[0], device_id_type=MESH)

    def relayed():
        for side in range(2):
            pl.semaphore_wait(relays.at[side], 1)

    for load in loads[2:]:
        load.start()

    used = count_ref[block]
    row32 = lax.broadcasted_iota(jnp.int32, (32, GRID), 0)
    active = jnp.where(band * 4 + row32 % 4 < used, 1.0, 0.0).astype(F32)
    orb_in.wait()
    for n in range(8):
        for c in range(2):
            piece = orb_ref[2 * n + c].astype(F32)
            wide[0, 32 * c + 4 * n : 32 * c + 4 * n + 4, :] = piece[:, 0:128]
            wide[1, 32 * c + 4 * n : 32 * c + 4 * n + 4, 0:64] = piece[:, 128:192]

    def wide_rows(rows):
        return jnp.concatenate([wide[h, rows, :] for h in range(2)], axis=1)[:, 0:GRID]

    real = wide_rows(slice(0, 32)) * active
    imag = wide_rows(slice(32, 64)) * active
    for start, part in ((0, real), (32, imag), (64, -real)):
        wide[0, start : start + 32, :] = part[:, 0:128]
        wide[1, start : start + 32, 0:64] = part[:, 128:192]
    real = real.astype(BF16)
    imag = imag.astype(BF16)
    ztab_in.wait()
    along_z = (
        dot(real, ztab_ref[0:192, :])
        + dot(real, ztab_ref[384:576, :])
        + dot(imag, ztab_ref[192:384, :])
        + dot(imag, ztab_ref[576:768, :])
    )
    for x in range(XN):
        for n in range(8):
            send_b[8 * x + n] = along_z[4 * n : 4 * n + 4, 128 * x : 128 * x + 128].astype(BF16)

    pl.semaphore_wait(barrier, peers + 7)
    relay()
    cols_b[0]()

    def slot_rows(slot, starts):
        parts = [wide_rows(pl.ds(start + slot, 8, stride=4)) for start in starts]
        return jnp.concatenate(parts, axis=0).astype(BF16)

    proj_in.wait()
    partial = jnp.zeros((16, 512), F32)
    for slot in range(4):
        partial += dot(slot_rows(slot, (0, 32)), proj_ref[slot * 192 : (slot + 1) * 192, :])
        partial += dot(slot_rows(slot, (32, 64)), proj_ref[(slot + 4) * 192 : (slot + 5) * 192, :])
    for x in range(XN):
        for c in range(2):
            send_pb[8 * x : 8 * x + 8, c, :] = partial[8 * c : 8 * c + 8, 128 * x : 128 * x + 128]
    proj_b[0]()

    stage[...] = jnp.zeros_like(stage)
    found[...] = jnp.zeros_like(found)
    grid_sum[...] = jnp.zeros_like(grid_sum)
    site_in.wait()

    def sources(t):
        return lax.rem(zz + ZN - t, ZN), lax.rem(zz + t + 1, ZN)

    rows = lax.broadcasted_iota(jnp.int32, (GRID, 128), 0)
    is_even = rows < 97
    frequency = jnp.where(is_even, rows, rows - 96)

    def folded(position):
        distance = jnp.minimum(position, GRID - position)
        sign = jnp.where(position < 96, 1.0, -1.0).astype(F32)
        return jnp.where(frequency == distance, jnp.where(is_even, 1.0, sign), 0.0).astype(BF16)

    @pl.loop(0, 8)
    def _(t):
        for h, s in enumerate(sources(t)):
            site = site_ref[pl.ds(s, 1), :]
            kx = (site * 43691) >> 23
            lanes = pl.ds(pl.multiple_of(t * 256 + h * 128, 128), 128)
            picks_x[:, lanes] = folded(kx)
            picks_y[:, lanes] = folded(site - kx * 192)

    recv_b[pl.ds(me, 1)] = send_b[pl.ds(me, 1)]
    cols_b[1]()
    for p in range(peers):
        turn[4 * p : 4 * p + 4, :] = recv_b[p].astype(F32)
    turned = turn[...].T
    for c in range(2):
        for zi in range(3):
            stage[pl.ds(c * 3 + zi, 16, stride=8), :] = turned[64 * c + 16 * zi : 64 * c + 16 * zi + 16]
    send_z[...] = stage[...].reshape(16, 8, 128).astype(BF16)
    relayed()
    cols_z_start()
    recv_z[pl.ds(zz, 1)] = send_z[pl.ds(zz, 1)]

    recv_pb[pl.ds(me, 1)] = send_pb[pl.ds(me, 1)]
    proj_b[1]()
    total = recv_pb[0]
    for p in range(1, peers):
        total += recv_pb[p]
    send_pz[...] = total
    recv_pz[pl.ds(zz, 1)] = total[None]
    proj_z[0]()

    atom_in.wait()
    coup_in.wait()
    atoms = lax.broadcasted_iota(jnp.int32, (64, 128), 0)
    marks = jnp.concatenate(
        [jnp.where(atoms == atom_ref[q : q + 1, :], 1.0, 0.0).astype(F32) for q in range(4)], axis=1
    )
    same = dot(marks.T.astype(BF16), marks.astype(BF16))
    coupled = jnp.where(same > 0.5, coup_ref[...], 0.0)
    part_h, part_l = split(coupled)
    coupled_h[...] = part_h
    coupled_l[...] = part_l

    def scatter(t):
        for h, s in enumerate(sources(t)):
            arrived = recv_z[s].astype(F32)
            spots = picks_x[:, pl.ds(pl.multiple_of(t * 256 + h * 128, 128), 128)]
            for i in range(6):
                row = (i % 2) * 3 + i // 2
                value = arrived[row : row + 1]
                spread = jnp.broadcast_to(value, (GRID, 128)).astype(BF16)
                weights[i * 192 : (i + 1) * 192, h * 128 : (h + 1) * 128] = spots * spread
        grid_sum[...] += dot_nt(weights[...], picks_y[:, pl.ds(pl.multiple_of(t * 256, 256), 256)])

    cols_z_wait(0, 1)
    scatter(0)

    @pl.loop(1, 8)
    def _(t):
        cols_z_wait(t, 2)
        scatter(t)

    cols_z_sent()

    plane_in.wait()
    pot_in.wait()
    across_h = plane_ref[0:192, :]
    across_l = plane_ref[192:384, :]
    down_h = plane_ref[384:576, :]
    down_l = plane_ref[576:768, :]
    scale = 1.0 / float(GRID**3)
    even_row = lax.broadcasted_iota(jnp.int32, (GRID, GRID), 0) < 97
    even_lane = lax.broadcasted_iota(jnp.int32, (GRID, GRID), 1) < 97

    def times_i(even, real, imag):
        return jnp.where(even, real, -imag), jnp.where(even, imag, real)

    def times_minus_i(even, real, imag):
        return jnp.where(even, real, imag), jnp.where(even, imag, -real)

    def from_left(first, value):
        high, low = split(value)
        both = dot(plane_ref[first : first + 384, :], high)
        return both[0:192] + both[192:384] + dot(plane_ref[first : first + 192, :], low)

    def from_right(real, imag, table_h, table_l):
        high, low = split(jnp.concatenate([real, imag], axis=0))
        both = dot(high, table_h) + dot(high, table_l) + dot(low, table_h)
        return both[0:192], both[192:384]

    def one_plane(zi):
        rows = pl.ds(pl.multiple_of(zi * 384, 384), 384)
        start = grid_sum[rows, :]
        real, imag = times_i(even_lane, start[0:192], start[192:384])
        real, imag = from_right(real, imag, down_h, down_l)
        real, imag = times_i(even_row, real, imag)
        field = pot_ref[zi] * scale
        real = from_left(0, real) * field
        imag = from_left(0, imag) * field
        real = from_left(384, real)
        imag = from_left(384, imag)
        real, imag = times_minus_i(even_row, real, imag)
        real, imag = from_right(real, imag, across_h, across_l)
        real, imag = times_minus_i(even_lane, real, imag)
        grid_back[rows, :] = jnp.concatenate([real, imag], axis=0).astype(BF16)

    one_plane(0)

    proj_z[1]()
    total = recv_pz[0]
    for z in range(1, ZN):
        total += recv_pz[z]
    back_pb[...] = total
    got_pb[pl.ds(me, 1)] = total[None]
    sums_b[0]()

    @pl.loop(1, 3)
    def _(zi):
        one_plane(zi)

    def gather(t):
        lanes = pl.ds(pl.multiple_of(t * 256, 256), 256)
        picked = dot(grid_back[...], picks_y[:, lanes])
        spots = picks_x[:, lanes].astype(F32)
        for i in range(6):
            value = jnp.sum(picked[i * 192 : (i + 1) * 192] * spots, axis=0, keepdims=True)
            for h in range(2):
                row = h * 8 + (i % 2) * 3 + i // 2
                found[row : row + 1, :] = value[:, h * 128 : (h + 1) * 128]
        for h, s in enumerate(sources(t)):
            back_z[s] = found[8 * h : 8 * h + 8, :]

    @pl.loop(0, 7)
    def _(i):
        t = 7 - i
        gather(t)
        home_z[2](t + 1)
        home_z[2](16 - t)

    gather(0)
    home_z[2](1)
    got_z[pl.ds(zz, 1)] = back_z[pl.ds(zz, 1)]

    sums_b[1]()
    pairs = []
    for part in range(4):
        real = got_pb[8 * part : 8 * part + 8, 0, :]
        imag = got_pb[8 * part : 8 * part + 8, 1, :]
        pairs.append(jnp.concatenate([real, imag, -imag, real], axis=0))
    high, low = split(jnp.concatenate(pairs, axis=1))
    weighted = dot_nt(high, coupled_h[...]) + dot_nt(high, coupled_l[...]) + dot_nt(low, coupled_h[...])
    weighted = weighted.astype(BF16)
    for slot in range(4):
        mixed = dot_nt(weighted[0:16], proj_ref[slot * 192 : (slot + 1) * 192, :]) + dot_nt(
            weighted[16:32], proj_ref[(slot + 4) * 192 : (slot + 5) * 192, :]
        )
        mixed = jnp.concatenate([mixed, jnp.zeros((16, 64), F32)], axis=1)
        for c in range(2):
            for h in range(2):
                wide[h, pl.ds(32 * c + slot, 8, stride=4), :] = mixed[8 * c : 8 * c + 8, 128 * h : 128 * h + 128]

    home_z[1]()
    stage[...] = got_z[...].reshape(128, 128)
    rows = []
    for c in range(2):
        rows += [stage[pl.ds(c * 3 + zi, 16, stride=8), :] for zi in range(3)]
        rows.append(jnp.zeros((16, 128), F32))
    turned = jnp.concatenate(rows, axis=0).T
    for p in range(peers):
        back_b[p] = turned[4 * p : 4 * p + 4]
    home_b[0]()
    got_b[pl.ds(me, 1)] = back_b[pl.ds(me, 1)]
    home_b[1]()
    for x in range(XN):
        for n in range(8):
            turn[32 * x + 4 * n : 32 * x + 4 * n + 4, :] = got_b[8 * x + n]
    wave = jnp.concatenate([turn[32 * x : 32 * x + 32, :] for x in range(XN)], axis=1)
    high, low = split(wave)
    for c in range(2):
        table_h = ztab_ref[192 * c : 192 * c + 192, :]
        local = dot_nt(high, table_h) + dot_nt(high, ztab_ref[192 * c + 384 : 192 * c + 576, :]) + dot_nt(low, table_h)
        result = (local + wide_rows(slice(32 * c, 32 * c + 32))) * active
        for n in range(8):
            out_ref[2 * n + c] = result[4 * n : 4 * n + 4, :]


def on_device(orbitals, projectors, potential, couplings, atom_index, column_site, column_count):
    plane, ztab = (jnp.asarray(t) for t in make_tables())
    vmem = pl.BlockSpec(memory_space=pltpu.VMEM)
    hbm = pl.BlockSpec(memory_space=pltpu.HBM)
    smem = pl.BlockSpec(memory_space=pltpu.SMEM)
    flat = projectors.transpose(1, 2, 3, 0).reshape(8 * GRID, 512)
    scratch = lambda *shape: pltpu.VMEM(shape, F32)
    out = pl.pallas_call(
        kernel,
        out_shape=pltpu.VMEM((16, 4, GRID), F32),
        in_specs=[smem] + [hbm] * 8,
        out_specs=vmem,
        scratch_shapes=[
            pltpu.VMEM((16, 128), jnp.int32),
            pltpu.VMEM((4, 128), jnp.int32),
            pltpu.VMEM((16, 4, GRID), BF16),
            pltpu.VMEM((8 * GRID, 512), BF16),
            scratch(3, GRID, GRID),
            scratch(512, 512),
            pltpu.VMEM((768, GRID), BF16),
            pltpu.VMEM((768, 512), BF16),
            scratch(2, 128, 128),
            pltpu.VMEM((32, 4, 128), BF16),
            pltpu.VMEM((32, 4, 128), BF16),
            scratch(32, 2, 128),
            scratch(32, 2, 128),
            scratch(128, 128),
            scratch(128, 128),
            pltpu.VMEM((16, 8, 128), BF16),
            pltpu.VMEM((16, 8, 128), BF16),
            scratch(2, 128),
            scratch(16, 2, 128),
            pltpu.VMEM((GRID, 2048), BF16),
            pltpu.VMEM((GRID, 2048), BF16),
            pltpu.VMEM((1152, 256), BF16),
            scratch(1152, GRID),
            pltpu.VMEM((1152, GRID), BF16),
            pltpu.VMEM((512, 512), BF16),
            pltpu.VMEM((512, 512), BF16),
            scratch(16, 128),
            scratch(16, 8, 128),
            scratch(16, 8, 128),
            scratch(32, 4, 128),
            scratch(32, 4, 128),
            scratch(2, 128),
            scratch(32, 2, 128),
            pltpu.SemaphoreType.DMA((22,)),
            pltpu.SemaphoreType.DMA((8,)),
            pltpu.SemaphoreType.REGULAR((2,)),
        ],
        compiler_params=pltpu.CompilerParams(
            collective_id=0, has_side_effects=True, vmem_limit_bytes=60000000
        ),
    )(
        column_count,
        column_site.reshape(16, 128),
        atom_index.reshape(4, 128),
        orbitals.reshape(16, 4, GRID),
        flat,
        potential,
        couplings,
        plane,
        ztab,
    )
    return out.reshape(8, 2, 4, GRID)


def solution(mesh):
    return jax.shard_map(
        on_device,
        mesh=mesh,
        in_specs=(
            P(None, None, ("ga", "band"), None),
            P(None, None, ("ga", "band"), None),
            P("ga", None, None),
            P(),
            P(),
            P(),
            P(),
        ),
        out_specs=P(None, None, ("ga", "band"), None),
        check_vma=False,
    )
```
